32 devices in a mesh: chan: 4 (over y, x), space: 4 (over z), rep: 2 (over core).
Axes of the slice: x: 2, y: 2, z: 4, core: 2. Of those that a mesh axis runs over, the one named last changes fastest.
Arguments:
- inputs: bfloat16 [2, 2, 16, 512, 128], P('rep', None, 'space', 'chan'), may hold values from -6 to 6
- grad_out: bfloat16 [2, 2, 16, 512, 128], P('rep', None, 'space', 'chan'), may hold values from -6 to 6
- weight: bfloat16 [3, 3, 3, 512, 512], P(None, None, None, 'chan'), may hold values from -0.0546875 to 0.0546875
Outputs:
- grad_in: bfloat16 [2, 2, 16, 512, 128], P('rep', None, 'space', 'chan')
- grad_weight: float32 [3, 3, 3, 512, 512], P(None, None, None, ('chan', 'rep'))
The draws below stay inside these ranges and needn't reach their ends.
All inputs are finite; a program needn't handle non-finite values.
Results may differ from the reference program's by a relative error of at most 0.0031.
Values may be sent and summed in bfloat16 or wider, within the bound.
A program may use at most 64 MiB of HBM per device.

```python
import jax
import jax.numpy as jnp

CIN = 512
COUT = 512
FRAMES = 2
WIDTH = 128
HEIGHT = 16
CLIPS = 2


def level_of(rng, extent, split, least, high):
    level = 1.0
    for dim, shards_of in split:
        heights = jax.random.uniform(jax.random.fold_in(jax.random.fold_in(rng, 6), dim), (shards_of,), jnp.float32, least / len(split), high / len(split))
        level = level * jnp.repeat(jnp.exp(heights), extent[dim] // shards_of).reshape((-1,) + (1,) * (len(extent) - 1 - dim))
    return level


def gaussian(stream_key, dims, width, most, split=(), kind=jnp.bfloat16):
    factor_of = level_of(stream_key, dims, split, -0.22, 0.18) if split else 1.0
    values = jax.random.normal(stream_key, dims, jnp.float32) * width * factor_of
    return jnp.minimum(jnp.maximum(values, -most), most).astype(kind)


def setup_inputs(seed: int = 0) -> dict:
    keys = jax.random.split(jax.random.key(seed), 4)
    return {
        "inputs": gaussian(keys[0], (CLIPS, FRAMES, HEIGHT, CIN, WIDTH), 1.0, 6.0, ((0, 2), (2, 4), (3, 4))),
        "grad_out": gaussian(keys[1], (CLIPS, FRAMES, HEIGHT, COUT, WIDTH), 1.0, 6.0, ((0, 2), (2, 4), (3, 4))),
        "weight": gaussian(keys[2], (3, 3, 3, COUT, CIN), (27 * CIN) ** -0.5, 0.0546875, ((3, 4),)),
    }


def reference(inputs, grad_out, weight):
    activated = jax.nn.silu(inputs.astype(jnp.float32)).astype(jnp.bfloat16)
    active_pad = jnp.pad(activated, ((0, 0), (2, 0), (1, 1), (0, 0), (1, 1))).astype(jnp.float32)
    grad_pad = jnp.pad(grad_out, ((0, 0), (0, 2), (1, 1), (0, 0), (1, 1))).astype(jnp.float32)
    grad_full = grad_out.astype(jnp.float32)
    weight_full = weight.astype(jnp.float32)
    clip_count, frame_count, row_count, in_width, col_count = inputs.shape
    active_grad = jnp.zeros(inputs.shape, jnp.float32)
    tap_terms = []
    for frame_tap in range(3):
        for row_tap in range(3):
            for col_tap in range(3):
                window = active_pad[:, frame_tap:frame_tap + frame_count, row_tap:row_tap + row_count, :, col_tap:col_tap + col_count]
                tap_terms.append(jnp.einsum("cthiw,cthow->oi", window, grad_full))
                shifted = grad_pad[:, 2 - frame_tap:2 - frame_tap + frame_count, 2 - row_tap:2 - row_tap + row_count, :, 2 - col_tap:2 - col_tap + col_count]
                active_grad = active_grad + jnp.einsum("cthow,oi->cthiw", shifted, weight_full[frame_tap, row_tap, col_tap])
    grad_weight = jnp.stack(tap_terms).reshape(3, 3, 3, grad_out.shape[3], in_width) * (1.0 / 256.0)
    values = inputs.astype(jnp.float32)
    logistic = jax.nn.sigmoid(values)
    slope = logistic * (1.0 + values * (1.0 - logistic))
    grad_in = (active_grad * slope).astype(jnp.bfloat16)
    return grad_in, grad_weight
```

```python
import functools

import jax
import jax.numpy as jnp
from jax import lax
from jax.experimental import pallas as pl
from jax.experimental.pallas import tpu as pltpu
from jax.sharding import PartitionSpec as P

MESH = pl.DeviceIdType.MESH
F32 = jnp.float32
BF16 = jnp.bfloat16
LANES = 128
LAG = 3


def flip(index, mask, count):
    out, bit = 0, 1
    while bit < count:
        out = out + (((index // bit) + ((mask // bit) % 2)) % 2) * bit
        bit *= 2
    return out


def nt(a, b):
    return lax.dot_general(a, b, (((1,), (1,)), ((), ())), preferred_element_type=F32)


def tn(a, b):
    return lax.dot_general(a, b, (((0,), (0,)), ((), ())), preferred_element_type=F32)


def taps_of(frames):
    return [(a, b) for b in (1, 0, 2) for a in range(max(0, 3 - frames), 3)]


def sizes_of(cfg):
    n_c, n_s, frames, rows, in_part, out_part, cols, in_all = cfg
    half = out_part // 2
    width = max(LANES, in_part)
    blocks = in_all // width
    chunk = 3 * half
    top = -(-(chunk // 2) // 16) * 16
    return half, width, blocks, width // in_part, chunk, top


def kernel(
    cfg,
    x_hbm, g_hbm, w_hbm,
    gi_ref, total,
    x_ref, g_ref, w_ref, act, halo, sib_halo, sib_rows, gd, gs,
    part, right_buf, left_buf, d_acc, d_out, d_one, d_two, d_mid,
    in_sem, g_send, g_recv, a_send, a_recv, b_send, b_recv,
    r_send, r_recv, l_send, l_recv, fr_send, fl_send, f_recv, d_send, d_recv,
):
    n_c, n_s, frames, rows, in_part, out_part, cols, in_all = cfg
    half, width, blocks, per, chunk, top = sizes_of(cfg)
    pairs = taps_of(frames)
    first = max(0, 3 - frames)
    plane = rows * cols
    deep = (rows + 2) * cols
    units = blocks * len(pairs)
    quad = n_c == 4

    chan = lax.axis_index("chan")
    space = lax.axis_index("space")
    rep = lax.axis_index("rep")
    other = 1 - rep
    has_left = space > 0
    has_right = space < n_s - 1
    after = (space + 1) % n_s
    before = (space + n_s - 1) % n_s

    def remote(src, dst, ssem, rsem, **where):
        return pltpu.make_async_remote_copy(
            src_ref=src, dst_ref=dst, send_sem=ssem, recv_sem=rsem,
            device_id=where, device_id_type=MESH,
        )

    loads = [
        pltpu.make_async_copy(x_hbm, x_ref, in_sem.at[0]),
        pltpu.make_async_copy(g_hbm, g_ref, in_sem.at[1]),
    ] + [
        pltpu.make_async_copy(w_hbm.at[pl.ds(first * 9, (3 - first) * 9), i], w_ref.at[i], in_sem.at[2 + i])
        for i in range(2)
    ]
    for load in loads:
        load.start()

    barrier = pltpu.get_barrier_semaphore()

    def greet(**where):
        pl.semaphore_signal(barrier, inc=1, device_id=where, device_id_type=MESH)

    peers = (1, 2) if quad else tuple(range(1, n_c))
    for k in peers:
        greet(chan=flip(chan, k, n_c))
    greet(rep=other)

    @pl.when(has_left)
    def _():
        greet(space=before)

    @pl.when(has_right)
    def _():
        greet(space=after)

    my_rows = pl.ds(pl.multiple_of(chan * in_part, in_part), in_part)
    loads[0].wait()
    for t in range(frames):
        for h in range(rows):
            v = x_ref[t, h].astype(F32)
            at = (t * rows + h) * cols
            act[0, my_rows, at : at + cols] = (v * jax.nn.sigmoid(v)).astype(BF16)

    def shifts(row):
        v = row.astype(F32)
        lane = lax.broadcasted_iota(jnp.int32, v.shape, 1)
        ahead = jnp.where(lane < cols - 1, pltpu.roll(v, cols - 1, 1), 0.0)
        behind = jnp.where(lane > 0, pltpu.roll(v, 1, 1), 0.0)
        return ahead.astype(BF16), row, behind.astype(BF16)

    def lay_own(t, p, row):
        at = (t * (rows + 2) + p) * cols
        moved = shifts(row)
        for e in range(3):
            for i in range(2):
                gd[i, e * half : (e + 1) * half, at : at + cols] = moved[e][i * half : (i + 1) * half]

    def lay_sib(t, p, row):
        at = (t * (rows + 2) + p) * cols
        moved = shifts(row)
        for e in range(3):
            gs[e * half : (e + 1) * half, at : at + cols] = moved[e]

    loads[1].wait()
    for t in range(frames):
        for h in range(rows):
            lay_own(t, h + 1, g_ref[t, h])

    met = len(peers) + 1
    inner = jnp.logical_and(has_left, has_right)

    @pl.when(inner)
    def _():
        pl.semaphore_wait(barrier, met + 2)

    @pl.when(jnp.logical_not(inner))
    def _():
        pl.semaphore_wait(barrier, met + (1 if n_s > 1 else 0))

    theirs = pl.ds(pl.multiple_of(other * half, half), half)

    def across():
        return remote(g_ref.at[:, :, theirs], sib_rows, g_send.at[0], g_recv.at[0], rep=other)

    def down():
        return remote(g_ref.at[:, rows - 1], halo.at[0], g_send.at[1], g_recv.at[1], space=after)

    def up():
        return remote(g_ref.at[:, 0], halo.at[1], g_send.at[2], g_recv.at[2], space=before)

    def down_sib():
        return remote(halo.at[0, :, theirs], sib_halo.at[0], g_send.at[3], g_recv.at[3], rep=other)

    def up_sib():
        return remote(halo.at[1, :, theirs], sib_halo.at[1], g_send.at[4], g_recv.at[4], rep=other)

    def chan_rows(k):
        owner = flip(chan, k, n_c)
        return pl.ds(pl.multiple_of(owner * in_part, in_part), in_part)

    def relay(k):
        return remote(act.at[0, chan_rows(k)], act.at[1, chan_rows(k)], b_send.at[k], b_recv.at[k], rep=other)

    def spread(k):
        return remote(act.at[0, my_rows], act.at[0, my_rows], a_send.at[k], a_recv.at[k], chan=flip(chan, k, n_c))

    def pass_on(i):
        span = in_part // 2
        src = flip(chan, 1 + i, n_c)
        where = pl.ds(pl.multiple_of(src * in_part + i * span, span), span)
        k = 0 if i == 0 else 3
        return remote(act.at[0, where], act.at[0, where], a_send.at[k], a_recv.at[k], chan=flip(chan, 2 - i, n_c))

    def pass_in(i):
        span = in_part // 2
        src = flip(chan, 3, n_c)
        where = pl.ds(pl.multiple_of(src * in_part + i * span, span), span)
        k = 0 if i == 0 else 3
        return remote(act.at[0, where], act.at[0, where], a_send.at[k], a_recv.at[k], chan=flip(chan, 2 - i, n_c))

    across().start()
    relay(0).start()

    @pl.when(has_right)
    def _():
        down().start()

    @pl.when(has_left)
    def _():
        up().start()

    for k in peers:
        spread(k).start()

    def block_of(j):
        return flip(chan // per, j, blocks)

    def produce(j, k):
        a, b = pairs[k]
        where = pl.ds(pl.multiple_of(block_of(j) * width, width), width)
        value = None
        for t in range(frames):
            to = t + 2 - a
            if to < frames:
                at = to * deep + (2 - b) * cols
                span = slice(t * plane, (t + 1) * plane)
                term = nt(gd[rep, :, at : at + plane], act[0, where, span])
                term = term + nt(gs[:, at : at + plane], act[1, where, span])
                value = term if value is None else value + term
        part[j * len(pairs) + k] = value

    def edges():
        @pl.when(has_left)
        def _():
            down().wait_recv()
            down_sib().start()

        @pl.when(jnp.logical_not(has_left))
        def _():
            halo[0] = jnp.zeros_like(halo[0])
            sib_halo[0] = jnp.zeros_like(sib_halo[0])

        @pl.when(has_right)
        def _():
            up().wait_recv()
            up_sib().start()

        @pl.when(jnp.logical_not(has_right))
        def _():
            halo[1] = jnp.zeros_like(halo[1])
            sib_halo[1] = jnp.zeros_like(sib_halo[1])

        for t in range(frames):
            for i in range(2):
                lay_own(t, i * (rows + 1), halo[i, t])

        @pl.when(has_left)
        def _():
            down_sib().wait_recv()

        @pl.when(has_right)
        def _():
            up_sib().wait_recv()

        for t in range(frames):
            for i in range(2):
                lay_sib(t, i * (rows + 1), sib_halo[i, t])

    def fetch(j):
        for k in range(j * per, (j + 1) * per):
            if k and quad and k == 3:
                pass_in(0).wait_recv()
                pass_in(1).wait_recv()
                relay(k).start()
            elif k:
                spread(k).wait_recv()
                relay(k).start()
                if quad:
                    pass_on(k - 1).start()

    def settle(j):
        for k in range(j * per, (j + 1) * per):
            relay(k).wait_recv()

    middle = max(1, n_s // 2)
    owners = (middle - 1, min(middle, n_s - 1))
    spans = (slice(0, top), slice(top, chunk))

    def far(i):
        return max(owners[i], n_s - 1 - owners[i])

    def go_right(u, i):
        return remote(right_buf.at[u, spans[i]], right_buf.at[u, spans[i]], r_send.at[u, i], r_recv.at[u, i], space=after)

    def go_left(u, i):
        return remote(left_buf.at[u, spans[i]], left_buf.at[u, spans[i]], l_send.at[u, i], l_recv.at[u, i], space=before)

    def final_right(u, i):
        return remote(total.at[u, spans[i]], total.at[u, spans[i]], fr_send.at[u, i], f_recv.at[u, i], space=after)

    def final_left(u, i):
        return remote(total.at[u, spans[i]], total.at[u, spans[i]], fl_send.at[u, i], f_recv.at[u, i], space=before)

    def live(u):
        return jnp.logical_and(u >= 0, u < units)

    def step_right(u, i):
        @pl.when(has_left)
        def _():
            go_right(u, i).wait_recv()
            right_buf[u, spans[i]] = (right_buf[u, spans[i]].astype(F32) + part[u, spans[i]]).astype(BF16)

        @pl.when(jnp.logical_not(has_left))
        def _():
            right_buf[u, spans[i]] = part[u, spans[i]].astype(BF16)

        go_right(u, i).start()

    def step_left(u, i):
        @pl.when(has_right)
        def _():
            go_left(u, i).wait_recv()
            left_buf[u, spans[i]] = (left_buf[u, spans[i]].astype(F32) + part[u, spans[i]]).astype(BF16)

        @pl.when(jnp.logical_not(has_right))
        def _():
            left_buf[u, spans[i]] = part[u, spans[i]].astype(BF16)

        go_left(u, i).start()

    def finish(u, i):
        value = part[u, spans[i]]
        if owners[i] > 0:
            go_right(u, i).wait_recv()
            value = value + right_buf[u, spans[i]].astype(F32)
        if owners[i] < n_s - 1:
            go_left(u, i).wait_recv()
            value = value + left_buf[u, spans[i]].astype(F32)
        total[u, spans[i]] = value.astype(BF16)
        if owners[i] > 0:
            final_left(u, i).start()
        if owners[i] < n_s - 1:
            final_right(u, i).start()

    def tick(time):
        for i in range(2):
            o = owners[i]
            right_unit = time - LAG * space
            left_unit = time - LAG * (n_s - 1 - space)
            done_unit = time - LAG * far(i)
            share_unit = time - LAG * (far(i) + jnp.maximum(space - o, o - space))

            @pl.when(jnp.logical_and(space < o, live(right_unit)))
            def _(i=i):
                step_right(right_unit, i)

            @pl.when(jnp.logical_and(space > o, live(left_unit)))
            def _(i=i):
                step_left(left_unit, i)

            @pl.when(jnp.logical_and(space == o, live(done_unit)))
            def _(i=i):
                finish(done_unit, i)

            @pl.when(jnp.logical_and(jnp.logical_and(space < o, has_left), live(share_unit)))
            def _(i=i):
                final_left(share_unit, i).wait_recv()
                final_left(share_unit, i).start()

            @pl.when(jnp.logical_and(jnp.logical_and(space > o, has_right), live(share_unit)))
            def _(i=i):
                final_right(share_unit, i).wait_recv()
                final_right(share_unit, i).start()

    def each(start, end, body):
        def run(i, carry):
            body(i)
            return carry

        lax.fori_loop(start, end, run, 0)

    def gather_last(u):
        for i in range(2):
            o = owners[i]

            @pl.when(jnp.logical_and(space != o, jnp.logical_or(space == 0, space == n_s - 1)))
            def _(i=i):
                final_left(u, i).wait_recv()

    def drain(u):
        for i in range(2):
            o = owners[i]

            @pl.when(space < o)
            def _(i=i):
                go_right(u, i).wait_send()

            @pl.when(space > o)
            def _(i=i):
                go_left(u, i).wait_send()

            @pl.when(jnp.logical_and(space >= o, has_right))
            def _(i=i):
                final_right(u, i).wait_send()

            @pl.when(jnp.logical_and(space <= o, has_left))
            def _(i=i):
                final_left(u, i).wait_send()

    def input_grad(t, i):
        where = slice(i * (in_all // 2), (i + 1) * (in_all // 2))
        value = None
        for a in range(first, 3):
            to = t + 2 - a
            if to < frames:
                for b in range(3):
                    at = to * deep + (2 - b) * cols
                    tap = ((a - first) * 3 + b) * 3
                    w = w_ref[:, tap : tap + 3, :, where].reshape(6 * half, in_all // 2)
                    term = tn(w, gd[:, :, at : at + plane].reshape(6 * half, plane))
                    value = term if value is None else value + term
        d_acc[t, where] = value
        d_out[t, where] = value.astype(BF16)

    def give(t, k):
        return remote(d_out.at[t, chan_rows(k)], d_one.at[t, k], d_send.at[t, k], d_recv.at[t, k], chan=flip(chan, k, n_c))

    def hop(t):
        return 1 + t % 2

    def give_one(t, k):
        block = hop(t) if k == 0 else 3
        return remote(
            d_out.at[t, chan_rows(block)], d_one.at[t, k], d_send.at[t, k], d_recv.at[t, k],
            chan=flip(chan, hop(t), n_c),
        )

    def give_two(t):
        return remote(d_mid.at[t], d_two.at[t], d_send.at[t, 2], d_recv.at[t, 2], chan=flip(chan, 3 - hop(t), n_c))

    def input_send(t):
        if quad:
            give_one(t, 1).start()
            give_one(t, 0).start()
        else:
            for k in peers:
                give(t, k).start()

    def input_mid(t):
        if quad:
            give_one(t, 1).wait_recv()
            d_mid[t] = (d_acc[t, chan_rows(3 - hop(t))] + d_one[t, 1].astype(F32)).astype(BF16)
            give_two(t).start()

    def input_end(t):
        if quad:
            give_one(t, 0).wait_recv()
            give_two(t).wait_recv()
        else:
            for k in peers:
                give(t, k).wait_recv()
        for h in range(rows):
            at = slice(h * cols, (h + 1) * cols)
            value = d_acc[t, my_rows, at]
            if quad:
                value = value + d_one[t, 0, :, at].astype(F32) + d_two[t, :, at].astype(F32)
            else:
                for k in peers:
                    value = value + d_one[t, k, :, at].astype(F32)
            v = x_ref[t, h].astype(F32)
            s = jax.nn.sigmoid(v)
            gi_ref[t, h] = (value * (s * (1.0 + v * (1.0 - s)))).astype(BF16)

    def input_sent(t):
        if quad:
            give_one(t, 0).wait_send()
            give_one(t, 1).wait_send()
            give_two(t).wait_send()
        else:
            for k in peers:
                give(t, k).wait_send()

    across().wait_recv()
    for t in range(frames):
        for h in range(rows):
            lay_sib(t, h + 1, sib_rows[t, h])

    count = len(pairs)
    spare = list(range(2 * frames))
    for j in range(blocks):
        settle(j)
        for k in range(count):
            if j == 0 and pairs[k][1] != 1 and pairs[k - 1][1] == 1:
                edges()
                loads[2].wait()
                loads[3].wait()
            produce(j, k)
            tick(j * count + k)
            if j == min(1, blocks - 1) and k < len(spare):
                t = frames - 1 - k // 2
                input_grad(t, k % 2)
                if k % 2:
                    input_send(t)
            if quad and blocks > 2 and j == 1 and k == count - 1:
                fetch(3)
            if j == blocks - 1 and k == 1:
                for t in reversed(range(frames)):
                    input_mid(t)
        if j + 1 < blocks:
            if not quad:
                fetch(j + 1)
            elif j == 0:
                fetch(1)
                fetch(2)

    reach = max(
        max([far(i) + abs(owners[i] - s) for s in range(1, n_s - 1)] + [far(i)]) for i in range(2)
    )
    tail = LAG * reach
    each(units, units + tail // 2, tick)
    for t in reversed(range(frames)):
        input_end(t)
    each(units + tail // 2, units + tail, tick)
    each(0, units, gather_last)

    @pl.when(has_right)
    def _():
        down().wait_send()
        up_sib().wait_send()

    @pl.when(has_left)
    def _():
        up().wait_send()
        down_sib().wait_send()

    across().wait_send()
    for k in range(n_c):
        relay(k).wait_send()
    for k in peers:
        spread(k).wait_send()
    if quad:
        pass_on(0).wait_send()
        pass_on(1).wait_send()
    for t in range(frames):
        input_sent(t)
    each(0, units, drain)


def write(cfg, gi_ref, total, gi_out, gw_out, stage, blank, sem):
    n_c, n_s, frames, rows, in_part, out_part, cols, in_all = cfg
    half, width, blocks, per, chunk, top = sizes_of(cfg)
    pairs = taps_of(frames)
    first = max(0, 3 - frames)
    chan = lax.axis_index("chan")
    copies = [pltpu.make_async_copy(gi_ref, gi_out, sem.at[0])]
    blank[...] = jnp.zeros_like(blank)
    for i in range(first * 3):
        copies.append(pltpu.make_async_copy(blank, gw_out.at[pl.ds(i * 3, 3)], sem.at[1 + i]))
    for copy in copies:
        copy.start()
    for k, (a, b) in enumerate(pairs):
        for j in range(blocks):
            block = flip(chan // per, j, blocks)
            value = total[j * len(pairs) + k].astype(F32) * (1.0 / 256.0)
            stage[k, :, :, pl.ds(pl.multiple_of(block * width, width), width)] = value.reshape(3, half, width)
        copies.append(pltpu.make_async_copy(stage.at[k], gw_out.at[pl.ds((a * 3 + b) * 3, 3)], sem.at[1 + a * 3 + b]))
        copies[-1].start()
    for copy in copies:
        copy.wait()


def on_device(sizes, inputs, grad_out, weight):
    n_c, n_s = sizes
    _, frames, rows, in_part, cols = inputs.shape
    out_part = grad_out.shape[3]
    in_all = weight.shape[4]
    cfg = (n_c, n_s, frames, rows, in_part, out_part, cols, in_all)
    half, width, blocks, per, chunk, top = sizes_of(cfg)
    pairs = taps_of(frames)
    taps = len(pairs) * 3
    plane = rows * cols
    cells = frames * plane
    lanes = frames * (rows + 2) * cols
    units = blocks * len(pairs)
    slots = max(3, n_c)
    dma = pltpu.SemaphoreType.DMA
    chunk_sem = dma((units, 2))
    vmem = pl.BlockSpec(memory_space=pltpu.VMEM)
    hbm = pl.BlockSpec(memory_space=pltpu.HBM)
    grad_in, total = pl.pallas_call(
        functools.partial(kernel, cfg),
        out_shape=(
            jax.ShapeDtypeStruct((frames, rows, in_part, cols), BF16),
            jax.ShapeDtypeStruct((units, chunk, width), BF16),
        ),
        in_specs=[hbm, hbm, hbm],
        out_specs=(vmem, vmem),
        scratch_shapes=[
            pltpu.VMEM((frames, rows, in_part, cols), BF16),
            pltpu.VMEM((frames, rows, out_part, cols), BF16),
            pltpu.VMEM((2, taps, half, in_all), BF16),
            pltpu.VMEM((2, in_all, cells), BF16),
            pltpu.VMEM((2, frames, out_part, cols), BF16),
            pltpu.VMEM((2, frames, half, cols), BF16),
            pltpu.VMEM((frames, rows, half, cols), BF16),
            pltpu.VMEM((2, 3 * half, lanes), BF16),
            pltpu.VMEM((3 * half, lanes), BF16),
            pltpu.VMEM((units, chunk, width), F32),
            pltpu.VMEM((units, chunk, width), BF16),
            pltpu.VMEM((units, chunk, width), BF16),
            pltpu.VMEM((frames, in_all, plane), F32),
            pltpu.VMEM((frames, in_all, plane), BF16),
            pltpu.VMEM((frames, slots, in_part, plane), BF16),
            pltpu.VMEM((frames, in_part, plane), BF16),
            pltpu.VMEM((frames, in_part, plane), BF16),
            dma((4,)),
            dma((5,)),
            dma((5,)),
            dma((max(4, n_c),)),
            dma((max(4, n_c),)),
            dma((n_c,)),
            dma((n_c,)),
            chunk_sem, chunk_sem, chunk_sem, chunk_sem, chunk_sem, chunk_sem, chunk_sem,
            dma((frames, slots)),
            dma((frames, slots)),
        ],
        compiler_params=pltpu.CompilerParams(
            collective_id=0, has_side_effects=True, vmem_limit_bytes=59 << 20
        ),
    )(
        inputs.reshape(frames, rows, in_part, cols),
        grad_out.reshape(frames, rows, out_part, cols),
        weight.reshape(27, 2, half, in_all),
    )
    grad_in, grad_weight = pl.pallas_call(
        functools.partial(write, cfg),
        out_shape=(
            jax.ShapeDtypeStruct((frames, rows, in_part, cols), BF16),
            jax.ShapeDtypeStruct((27, half, in_all), F32),
        ),
        in_specs=[vmem, vmem],
        out_specs=(hbm, hbm),
        scratch_shapes=[
            pltpu.VMEM((len(pairs), 3, half, in_all), F32),
            pltpu.VMEM((3, half, in_all), F32),
            dma((10,)),
        ],
        compiler_params=pltpu.CompilerParams(vmem_limit_bytes=24 << 20),
    )(grad_in, total)
    return grad_in.reshape(inputs.shape), grad_weight.reshape(3, 3, 3, half, in_all)


def solution(mesh):
    return jax.shard_map(
        functools.partial(on_device, (mesh.shape["chan"], mesh.shape["space"])),
        mesh=mesh,
        in_specs=(
            P("rep", None, "space", "chan", None),
            P("rep", None, "space", "chan", None),
            P(None, None, None, "chan", None),
        ),
        out_specs=(
            P("rep", None, "space", "chan", None),
            P(None, None, None, ("chan", "rep"), None),
        ),
        check_vma=False,
    )
```

```python
import functools

import jax
import jax.numpy as jnp
from jax import lax
from jax.experimental import pallas as pl
from jax.experimental.pallas import tpu as pltpu
from jax.sharding import PartitionSpec as P

MESH = pl.DeviceIdType.MESH
F32 = jnp.float32
BF16 = jnp.bfloat16
LANES = 128
LAG_SUM = 8
LAG_DONE = 7
GRAD_AT = 3


def flip(index, mask, count):
    out, bit = 0, 1
    while bit < count:
        out = out + (((index // bit) + ((mask // bit) % 2)) % 2) * bit
        bit *= 2
    return out


def nt(a, b):
    return lax.dot_general(a, b, (((1,), (1,)), ((), ())), preferred_element_type=F32)


def nn(a, b):
    return lax.dot_general(a, b, (((1,), (0,)), ((), ())), preferred_element_type=F32)


def taps_of(frames):
    return [(a, b) for b in (1, 0, 2) for a in range(max(0, 3 - frames), 3)]


def sizes_of(cfg):
    n_c, n_s, frames, rows, in_part, out_part, cols, in_all = cfg
    half = out_part // 2
    width = max(LANES, in_part)
    blocks = in_all // width
    chunk = 3 * half
    split = 2 if chunk % 32 == 0 else 1
    return half, width, blocks, width // in_part, chunk, split


def order_of(cfg):
    half, width, blocks, per, chunk, split = sizes_of(cfg)
    pairs = taps_of(cfg[2])
    every = range(len(pairs))
    if cfg[0] != 4:
        return [(j, k) for j in range(blocks) for k in every]
    low = [k for k in every if pairs[k][0] < 2]
    high = [k for k in every if pairs[k][0] == 2]
    order = [(0, k) for k in every]
    for group in ((1, 2), (3,)):
        for part in (low, high):
            order += [(j, k) for j in group for k in part]
    return order


def kernel(
    cfg,
    x_hbm, g_hbm, w_hbm,
    gi_hbm, total_hbm,
    gi_ref, total, x_ref, g_ref, w_ref, wt_ref, g3, act, halo, sib_halo, sib_rows, gd, gs,
    part, sums, inbox, d_acc, d_out, d_one, d_two, d_mid,
    in_sem, out_sem, g_send, g_recv, c_send, c_recv, a_send, a_recv, p_send, p_recv, b_send, b_recv,
    s_send, s_recv, f_send, f_recv, d_send, d_recv,
):
    n_c, n_s, frames, rows, in_part, out_part, cols, in_all = cfg
    half, width, blocks, per, chunk, split = sizes_of(cfg)
    pairs = taps_of(frames)
    order = order_of(cfg)
    first = max(0, 3 - frames)
    plane = rows * cols
    deep = (rows + 2) * cols
    units = len(order)
    pieces = units * split
    piece = chunk // split
    quad = n_c == 4

    chan = lax.axis_index("chan")
    space = lax.axis_index("space")
    rep = lax.axis_index("rep")
    other = 1 - rep
    has_left = space > 0
    has_right = space < n_s - 1
    after = (space + 1) % n_s
    below = (space + n_s - 1) % n_s

    def remote(src, dst, ssem, rsem, **where):
        return pltpu.make_async_remote_copy(
            src_ref=src, dst_ref=dst, send_sem=ssem, recv_sem=rsem,
            device_id=where, device_id_type=MESH,
        )

    loads = [
        pltpu.make_async_copy(x_hbm, x_ref, in_sem.at[0]),
        pltpu.make_async_copy(g_hbm, g_ref, in_sem.at[1]),
    ] + [
        pltpu.make_async_copy(w_hbm.at[pl.ds(first * 9, (3 - first) * 9), i], w_ref.at[i], in_sem.at[2 + i])
        for i in range(2)
    ]
    for load in loads:
        load.start()

    barrier = pltpu.get_barrier_semaphore()

    def greet(**where):
        pl.semaphore_signal(barrier, inc=1, device_id=where, device_id_type=MESH)

    peers = (1, 2) if quad else tuple(range(1, n_c))
    for k in peers:
        greet(chan=flip(chan, k, n_c))
    greet(rep=other)

    @pl.when(has_left)
    def _():
        greet(space=below)

    @pl.when(has_right)
    def _():
        greet(space=after)

    my_rows = pl.ds(pl.multiple_of(chan * in_part, in_part), in_part)
    loads[0].wait()
    for t in range(frames):
        for h in range(rows):
            v = x_ref[t, h].astype(F32)
            at = h * cols
            act[0, t, my_rows, at : at + cols] = (v * jax.nn.sigmoid(v)).astype(BF16)

    def shifts(row):
        v = row.astype(F32)
        lane = lax.broadcasted_iota(jnp.int32, v.shape, 1)
        ahead = jnp.where(lane < cols - 1, pltpu.roll(v, cols - 1, 1), 0.0)
        behind = jnp.where(lane > 0, pltpu.roll(v, 1, 1), 0.0)
        return ahead.astype(BF16), row, behind.astype(BF16)

    def lay_own(t, p, row):
        at = (t * (rows + 2) + p) * cols
        moved = shifts(row)
        for e in range(3):
            for i in range(2):
                gd[i, e * half : (e + 1) * half, at : at + cols] = moved[e][i * half : (i + 1) * half]

    def lay_sib(t, p, row):
        at = (t * (rows + 2) + p) * cols
        moved = shifts(row)
        for e in range(3):
            gs[e * half : (e + 1) * half, at : at + cols] = moved[e]

    loads[1].wait()
    for t in range(frames):
        for h in range(rows):
            lay_own(t, h + 1, g_ref[t, h])

    met = len(peers) + 1
    both = jnp.logical_and(has_left, has_right)

    @pl.when(both)
    def _():
        pl.semaphore_wait(barrier, met + 2)

    @pl.when(jnp.logical_not(both))
    def _():
        pl.semaphore_wait(barrier, met + (1 if n_s > 1 else 0))

    theirs = pl.ds(pl.multiple_of(other * half, half), half)

    def across(t):
        return remote(g_ref.at[t, :, theirs], sib_rows.at[t], c_send.at[t], c_recv.at[t], rep=other)

    def down():
        return remote(g_ref.at[:, rows - 1], halo.at[0], g_send.at[1], g_recv.at[1], space=after)

    def up():
        return remote(g_ref.at[:, 0], halo.at[1], g_send.at[2], g_recv.at[2], space=below)

    def down_sib():
        return remote(halo.at[0, :, theirs], sib_halo.at[0], g_send.at[3], g_recv.at[3], rep=other)

    def up_sib():
        return remote(halo.at[1, :, theirs], sib_halo.at[1], g_send.at[4], g_recv.at[4], rep=other)

    def chan_rows(k):
        owner = flip(chan, k, n_c)
        return pl.ds(pl.multiple_of(owner * in_part, in_part), in_part)

    def relay(k, t):
        return remote(act.at[0, t, chan_rows(k)], act.at[1, t, chan_rows(k)], b_send.at[k, t], b_recv.at[k, t], rep=other)

    def spread(k, t):
        return remote(act.at[0, t, my_rows], act.at[0, t, my_rows], a_send.at[k, t], a_recv.at[k, t], chan=flip(chan, k, n_c))

    def half_rows(k, i):
        span = in_part // 2
        return pl.ds(pl.multiple_of(flip(chan, k, n_c) * in_part + i * span, span), span)

    def pass_on(i, t):
        where = half_rows(1 + i, i)
        return remote(act.at[0, t, where], act.at[0, t, where], p_send.at[i, t], p_recv.at[i, t], chan=flip(chan, 2 - i, n_c))

    def pass_in(i, t):
        where = half_rows(3, i)
        return remote(act.at[0, t, where], act.at[0, t, where], p_send.at[i, t], p_recv.at[i, t], chan=flip(chan, 2 - i, n_c))

    for t in range(frames):
        across(frames - 1 - t).start()
        relay(0, t).start()

    @pl.when(has_right)
    def _():
        down().start()

    @pl.when(has_left)
    def _():
        up().start()

    for t in range(frames):
        for k in peers:
            spread(k, t).start()

    def block_of(j):
        return flip(chan // per, j, blocks)

    def produce(n):
        j, k = order[n]
        a, b = pairs[k]
        where = pl.ds(pl.multiple_of(block_of(j) * width, width), width)
        value = None
        for t in range(frames):
            to = t + 2 - a
            if to < frames:
                at = to * deep + (2 - b) * cols
                term = nt(gd[rep, :, at : at + plane], act[0, t, where])
                term = term + nt(gs[:, at : at + plane], act[1, t, where])
                value = term if value is None else value + term
        for i in range(split):
            part[n * split + i] = value[i * piece : (i + 1) * piece]

    def edges():
        @pl.when(has_left)
        def _():
            down().wait_recv()
            down_sib().start()

        @pl.when(jnp.logical_not(has_left))
        def _():
            halo[0] = jnp.zeros_like(halo[0])
            sib_halo[0] = jnp.zeros_like(sib_halo[0])

        @pl.when(has_right)
        def _():
            up().wait_recv()
            up_sib().start()

        @pl.when(jnp.logical_not(has_right))
        def _():
            halo[1] = jnp.zeros_like(halo[1])
            sib_halo[1] = jnp.zeros_like(sib_halo[1])

        for t in range(frames):
            for i in range(2):
                lay_own(t, i * (rows + 1), halo[i, t])

        @pl.when(has_left)
        def _():
            down_sib().wait_recv()

        @pl.when(has_right)
        def _():
            up_sib().wait_recv()

        for t in range(frames):
            for i in range(2):
                lay_sib(t, i * (rows + 1), sib_halo[i, t])

    def fetch(j, t):
        for k in range(j * per, (j + 1) * per):
            if quad and k == 3:
                pass_in(0, t).wait_recv()
                pass_in(1, t).wait_recv()
            elif k:
                spread(k, t).wait_recv()
            if k:
                relay(k, t).start()
            if quad and k in (1, 2):
                pass_on(k - 1, t).start()

    def settle(j, t):
        for k in range(j * per, (j + 1) * per):
            relay(k, t).wait_recv()

    middle = n_s // 2
    on_left = space < middle
    inner = jnp.where(on_left, space + 1, space - 1)
    outer = jnp.clip(jnp.where(on_left, space - 1, space + 1), 0, n_s - 1)
    depth = jnp.where(on_left, space, n_s - 1 - space)
    gap = jnp.where(on_left, middle - 1 - space, space - middle)
    central = gap == 0
    has_outer = depth > 0
    deepest = max(middle - 1, n_s - 1 - middle, 0)
    box = jnp.where(central, 1, 0)

    def send_sum(q):
        return remote(sums.at[q], inbox.at[box, q], s_send, s_recv.at[box, q], space=inner)

    def from_outer(q):
        return remote(sums.at[q], inbox.at[0, q], s_send, s_recv.at[0, q], space=inner)

    def from_peer(q):
        return remote(sums.at[q], inbox.at[1, q], s_send, s_recv.at[1, q], space=inner)

    def send_done(q):
        return remote(total.at[q], total.at[q], f_send, f_recv.at[q], space=outer)

    def keep(q):
        return pltpu.make_async_copy(total.at[q], total_hbm.at[q], out_sem.at[0])

    def live(q):
        return jnp.logical_and(q >= 0, q < pieces)

    def tick(time):
        sum_piece = time - LAG_SUM * depth
        done_piece = time - LAG_SUM * deepest - LAG_DONE * (1 + gap)

        @pl.when(live(sum_piece))
        def _():
            @pl.when(has_outer)
            def _():
                from_outer(sum_piece).wait_recv()
                sums[sum_piece] = (part[sum_piece] + inbox[0, sum_piece].astype(F32)).astype(BF16)

            @pl.when(jnp.logical_not(has_outer))
            def _():
                sums[sum_piece] = part[sum_piece].astype(BF16)

            if n_s > 1:
                send_sum(sum_piece).start()

        @pl.when(jnp.logical_and(jnp.logical_or(central, has_outer), live(done_piece)))
        def _():
            @pl.when(central)
            def _():
                value = sums[done_piece]
                if n_s > 1:
                    from_peer(done_piece).wait_recv()
                    value = (value.astype(F32) + inbox[1, done_piece].astype(F32)).astype(BF16)
                total[done_piece] = value

            @pl.when(jnp.logical_not(central))
            def _():
                send_done(done_piece).wait_recv()

            @pl.when(has_outer)
            def _():
                send_done(done_piece).start()

            keep(done_piece).start()

    def each(start, end, body):
        def run(i, carry):
            body(i)
            return carry

        lax.fori_loop(start, end, run, 0)

    def last(q):
        send_done(q).wait_recv()
        keep(q).start()

    def line_up(t):
        for b in range(3):
            at = t * deep + (2 - b) * cols
            g3[t, b * 6 * half : (b + 1) * 6 * half] = gd[:, :, at : at + plane].reshape(6 * half, plane)

    def input_grad(t, i, cuts):
        size = plane // cuts
        where = slice(i * size, (i + 1) * size)
        value = None
        for a in range(first, 3):
            to = t + 2 - a
            if to < frames:
                term = nn(wt_ref[a - first], g3[to, :, where])
                value = term if value is None else value + term
        d_acc[t, :, where] = value
        d_out[t, :, where] = value.astype(BF16)

    def give(t, k):
        return remote(d_out.at[t, chan_rows(k)], d_one.at[t, k], d_send.at[t, k], d_recv.at[t, k], chan=flip(chan, k, n_c))

    def hop(t):
        return 1 + t % 2

    def give_one(t, k):
        block = hop(t) if k == 0 else 3
        return remote(
            d_out.at[t, chan_rows(block)], d_one.at[t, k], d_send.at[t, k], d_recv.at[t, k],
            chan=flip(chan, hop(t), n_c),
        )

    def give_two(t):
        return remote(d_mid.at[t], d_two.at[t], d_send.at[t, 2], d_recv.at[t, 2], chan=flip(chan, 3 - hop(t), n_c))

    def input_send(t):
        if quad:
            give_one(t, 1).start()
            give_one(t, 0).start()
        else:
            for k in peers:
                give(t, k).start()

    def input_mid(t):
        if quad:
            give_one(t, 1).wait_recv()
            d_mid[t] = (d_acc[t, chan_rows(3 - hop(t))] + d_one[t, 1].astype(F32)).astype(BF16)
            give_two(t).start()

    def input_end(t):
        if quad:
            give_one(t, 0).wait_recv()
            give_two(t).wait_recv()
        else:
            for k in peers:
                give(t, k).wait_recv()
        for h in range(rows):
            at = slice(h * cols, (h + 1) * cols)
            value = d_acc[t, my_rows, at]
            if quad:
                value = value + d_one[t, 0, :, at].astype(F32) + d_two[t, :, at].astype(F32)
            else:
                for k in peers:
                    value = value + d_one[t, k, :, at].astype(F32)
            v = x_ref[t, h].astype(F32)
            s = jax.nn.sigmoid(v)
            gi_ref[t, h] = (value * (s * (1.0 + v * (1.0 - s)))).astype(BF16)

    def input_sent(t):
        if quad:
            give_one(t, 0).wait_send()
            give_one(t, 1).wait_send()
            give_two(t).wait_send()
        else:
            for k in peers:
                give(t, k).wait_send()

    def inside(t):
        across(t).wait_recv()
        for h in range(rows):
            lay_sib(t, h + 1, sib_rows[t, h])

    def turn():
        loads[2].wait()
        loads[3].wait()
        for tap in range((3 - first) * 3):
            a, b = tap // 3, tap % 3
            wt_ref[a, :, b * 6 * half : (b + 1) * 6 * half] = w_ref[:, tap * 3 : tap * 3 + 3].reshape(6 * half, in_all).T

    before = {}
    turn()

    def at_unit(n, act_now):
        before.setdefault(n, []).append(act_now)

    def grad_part(t, i, cuts):
        if i == 0:
            line_up(t)
        input_grad(t, i, cuts)
        if i == cuts - 1:
            input_send(t)

    at_unit(0, functools.partial(inside, frames - 1))
    at_unit(0, functools.partial(settle, 0, 0))
    for t in range(1, frames):
        at_unit(1, functools.partial(inside, frames - 1 - t))
        at_unit(1, functools.partial(settle, 0, t))
    count = len(pairs)
    cuts = 2
    for t in reversed(range(frames)):
        for c in range(cuts):
            at_unit(GRAD_AT, functools.partial(grad_part, t, c, cuts))
    if quad:
        for t in range(frames):
            early = t < frames - 1
            for j in (1, 2):
                at_unit(count - 1 if early else count + 3, functools.partial(fetch, j, t))
            for j in (1, 2):
                at_unit(count if early else 2 * count, functools.partial(settle, j, t))
            at_unit(2 * count + 3, functools.partial(fetch, 3, t))
            at_unit(3 * count, functools.partial(settle, 3, t))
    else:
        for j in range(1, blocks):
            for t in range(frames):
                at_unit(j * count, functools.partial(fetch, j, t))
            for t in range(frames):
                at_unit(j * count, functools.partial(settle, j, t))
    for t in reversed(range(frames)):
        at_unit(units - 4, functools.partial(input_mid, t))

    for n in range(units):
        if n == 3 - first:
            edges()
        for act_now in before.get(n, []):
            act_now()
        produce(n)
        for i in range(split):
            tick(n * split + i)
    each(pieces, pieces + LAG_SUM * deepest + LAG_DONE * (1 + deepest), tick)
    for t in reversed(range(frames)):
        input_end(t)
    pltpu.make_async_copy(gi_ref, gi_hbm, out_sem.at[1]).start()

    @pl.when(jnp.logical_not(jnp.logical_or(central, has_outer)))
    def _():
        each(0, pieces, last)

    @pl.when(has_right)
    def _():
        down().wait_send()
        up_sib().wait_send()

    @pl.when(has_left)
    def _():
        up().wait_send()
        down_sib().wait_send()

    for t in range(frames):
        across(t).wait_send()
        for k in range(n_c):
            relay(k, t).wait_send()
        for k in peers:
            spread(k, t).wait_send()
        if quad:
            pass_on(0, t).wait_send()
            pass_on(1, t).wait_send()
        input_sent(t)
    if n_s > 1:
        remote(sums, inbox.at[0], s_send, s_recv.at[0, 0], space=inner).wait_send()

    @pl.when(has_outer)
    def _():
        remote(total, total, f_send, f_recv.at[0], space=outer).wait_send()

    pltpu.make_async_copy(total, total_hbm, out_sem.at[0]).wait()
    pltpu.make_async_copy(gi_ref, gi_hbm, out_sem.at[1]).wait()


def write(cfg, gi_in, total_hbm, gi_out, gw_out, gi_ref, total, stage, blank, in_sem, sem):
    n_c, n_s, frames, rows, in_part, out_part, cols, in_all = cfg
    half, width, blocks, per, chunk, split = sizes_of(cfg)
    pairs = taps_of(frames)
    order = order_of(cfg)
    first = max(0, 3 - frames)
    chan = lax.axis_index("chan")
    ranked = sorted(range(len(order)), key=lambda n: (order[n][1], n))
    loads = []
    for n in ranked:
        some = pl.ds(n * split, split)
        loads.append(pltpu.make_async_copy(total_hbm.at[some], total.at[some], in_sem.at[n]))
    loads.append(pltpu.make_async_copy(gi_in, gi_ref, in_sem.at[len(order)]))
    for load in loads:
        load.start()
    blank[...] = jnp.zeros_like(blank)
    copies = []
    for i in range(first * 3):
        copies.append(pltpu.make_async_copy(blank, gw_out.at[pl.ds(i * 3, 3)], sem.at[1 + i]))
        copies[-1].start()
    for i, n in enumerate(ranked):
        loads[i].wait()
        j, k = order[n]
        a, b = pairs[k]
        where = pl.ds(pl.multiple_of(flip(chan // per, j, blocks) * width, width), width)
        value = total[n * split : (n + 1) * split].astype(F32) * (1.0 / 256.0)
        stage[k, :, :, where] = value.reshape(3, half, width)
        if (i + 1) % blocks == 0:
            copies.append(pltpu.make_async_copy(stage.at[k], gw_out.at[pl.ds((a * 3 + b) * 3, 3)], sem.at[1 + a * 3 + b]))
            copies[-1].start()
    loads[-1].wait()
    copies.append(pltpu.make_async_copy(gi_ref, gi_out, sem.at[0]))
    copies[-1].start()
    for copy in copies:
        copy.wait()


def on_device(sizes, inputs, grad_out, weight):
    n_c, n_s = sizes
    _, frames, rows, in_part, cols = inputs.shape
    out_part = grad_out.shape[3]
    in_all = weight.shape[4]
    cfg = (n_c, n_s, frames, rows, in_part, out_part, cols, in_all)
    half, width, blocks, per, chunk, split = sizes_of(cfg)
    pairs = taps_of(frames)
    taps = len(pairs) * 3
    plane = rows * cols
    lanes = frames * (rows + 2) * cols
    units = blocks * len(pairs)
    slots = max(3, n_c)
    dma = pltpu.SemaphoreType.DMA
    pieces = units * split
    pile = (pieces, chunk // split, width)
    hbm = pl.BlockSpec(memory_space=pltpu.HBM)
    grad_in, total = pl.pallas_call(
        functools.partial(kernel, cfg),
        out_shape=(
            jax.ShapeDtypeStruct((frames, rows, in_part, cols), BF16),
            jax.ShapeDtypeStruct(pile, BF16),
        ),
        in_specs=[hbm, hbm, hbm],
        out_specs=(hbm, hbm),
        scratch_shapes=[
            pltpu.VMEM((frames, rows, in_part, cols), BF16),
            pltpu.VMEM(pile, BF16),
            pltpu.VMEM((frames, rows, in_part, cols), BF16),
            pltpu.VMEM((frames, rows, out_part, cols), BF16),
            pltpu.VMEM((2, taps, half, in_all), BF16),
            pltpu.VMEM((taps // 9, in_all, 18 * half), BF16),
            pltpu.VMEM((frames, 18 * half, plane), BF16),
            pltpu.VMEM((2, frames, in_all, plane), BF16),
            pltpu.VMEM((2, frames, out_part, cols), BF16),
            pltpu.VMEM((2, frames, half, cols), BF16),
            pltpu.VMEM((frames, rows, half, cols), BF16),
            pltpu.VMEM((2, 3 * half, lanes), BF16),
            pltpu.VMEM((3 * half, lanes), BF16),
            pltpu.VMEM(pile, F32),
            pltpu.VMEM(pile, BF16),
            pltpu.VMEM((2,) + pile, BF16),
            pltpu.VMEM((frames, in_all, plane), F32),
            pltpu.VMEM((frames, in_all, plane), BF16),
            pltpu.VMEM((frames, slots, in_part, plane), BF16),
            pltpu.VMEM((frames, in_part, plane), BF16),
            pltpu.VMEM((frames, in_part, plane), BF16),
            dma((4,)),
            dma((2,)),
            dma((5,)),
            dma((5,)),
            dma((frames,)),
            dma((frames,)),
            dma((n_c, frames)),
            dma((n_c, frames)),
            dma((2, frames)),
            dma((2, frames)),
            dma((n_c, frames)),
            dma((n_c, frames)),
            dma,
            dma((2, pieces)),
            dma,
            dma((pieces,)),
            dma((frames, slots)),
            dma((frames, slots)),
        ],
        compiler_params=pltpu.CompilerParams(
            collective_id=0, has_side_effects=True, vmem_limit_bytes=59 << 20
        ),
    )(
        inputs.reshape(frames, rows, in_part, cols),
        grad_out.reshape(frames, rows, out_part, cols),
        weight.reshape(27, 2, half, in_all),
    )
    grad_in, grad_weight = pl.pallas_call(
        functools.partial(write, cfg),
        out_shape=(
            jax.ShapeDtypeStruct((frames, rows, in_part, cols), BF16),
            jax.ShapeDtypeStruct((27, half, in_all), F32),
        ),
        in_specs=[hbm, hbm],
        out_specs=(hbm, hbm),
        scratch_shapes=[
            pltpu.VMEM((frames, rows, in_part, cols), BF16),
            pltpu.VMEM(pile, BF16),
            pltpu.VMEM((len(pairs), 3, half, in_all), F32),
            pltpu.VMEM((3, half, in_all), F32),
            dma((units + 1,)),
            dma((10,)),
        ],
        compiler_params=pltpu.CompilerParams(vmem_limit_bytes=59 << 20),
    )(grad_in, total)
    return grad_in.reshape(inputs.shape), grad_weight.reshape(3, 3, 3, half, in_all)


def solution(mesh):
    return jax.shard_map(
        functools.partial(on_device, (mesh.shape["chan"], mesh.shape["space"])),
        mesh=mesh,
        in_specs=(
            P("rep", None, "space", "chan", None),
            P("rep", None, "space", "chan", None),
            P(None, None, None, "chan", None),
        ),
        out_specs=(
            P("rep", None, "space", "chan", None),
            P(None, None, None, ("chan", "rep"), None),
        ),
        check_vma=False,
    )
```

```python
import functools

import jax
import jax.numpy as jnp
from jax import lax
from jax.experimental import pallas as pl
from jax.experimental.pallas import tpu as pltpu
from jax.sharding import PartitionSpec as P

MESH = pl.DeviceIdType.MESH
F32 = jnp.float32
BF16 = jnp.bfloat16
LANES = 128
LAG_SUM = 5
LAG_DONE = 7


def flip(index, mask, count):
    out, bit = 0, 1
    while bit < count:
        out = out + (((index // bit) + ((mask // bit) % 2)) % 2) * bit
        bit *= 2
    return out


def nt(a, b):
    return lax.dot_general(a, b, (((1,), (1,)), ((), ())), preferred_element_type=F32)


def nn(a, b):
    return lax.dot_general(a, b, (((1,), (0,)), ((), ())), preferred_element_type=F32)


def taps_of(frames):
    taps = range(max(0, 3 - frames), 3)
    return [(a, 1) for a in taps] + [(a, b) for a in taps for b in (0, 2)]


def sizes_of(cfg):
    n_c, n_s, frames, rows, in_part, out_part, cols, in_all = cfg
    half = out_part // 2
    width = max(LANES, in_part)
    blocks = in_all // width
    chunk = 3 * half
    split = 2 if chunk % 32 == 0 else 1
    return half, width, blocks, width // in_part, chunk, split


def order_of(cfg):
    half, width, blocks, per, chunk, split = sizes_of(cfg)
    pairs = taps_of(cfg[2])
    every = range(len(pairs))
    if cfg[0] != 4:
        return [(j, k) for j in range(blocks) for k in every]
    low = [k for k in every if pairs[k][0] < 2]
    high = [k for k in every if pairs[k][0] == 2]
    order = [(0, k) for k in every]
    for group in ((1, 2), (3,)):
        for part in (low, high):
            order += [(j, k) for j in group for k in part]
    return order


def kernel(
    cfg,
    x_hbm, g_hbm, w_hbm,
    gi_hbm, total_hbm,
    gi_ref, total, x_ref, g_ref, w_ref, wt_ref, g3, act, halo, sib_halo, sib_rows, gd, gs,
    part, sums, inbox, d_acc, d_out, d_one, d_two, d_mid,
    in_sem, out_sem, g_send, g_recv, c_send, c_recv, a_send, a_recv, p_send, p_recv, b_send, b_recv,
    s_send, s_recv, f_send, f_recv, d_send, d_recv,
):
    n_c, n_s, frames, rows, in_part, out_part, cols, in_all = cfg
    half, width, blocks, per, chunk, split = sizes_of(cfg)
    pairs = taps_of(frames)
    order = order_of(cfg)
    first = max(0, 3 - frames)
    plane = rows * cols
    deep = (rows + 2) * cols
    units = len(order)
    pieces = units * split
    piece = chunk // split
    quad = n_c == 4

    chan = lax.axis_index("chan")
    space = lax.axis_index("space")
    rep = lax.axis_index("rep")
    other = 1 - rep
    has_left = space > 0
    has_right = space < n_s - 1
    after = (space + 1) % n_s
    below = (space + n_s - 1) % n_s

    def remote(src, dst, ssem, rsem, **where):
        return pltpu.make_async_remote_copy(
            src_ref=src, dst_ref=dst, send_sem=ssem, recv_sem=rsem,
            device_id=where, device_id_type=MESH,
        )

    loads = [
        pltpu.make_async_copy(x_hbm, x_ref, in_sem.at[0]),
        pltpu.make_async_copy(g_hbm, g_ref, in_sem.at[1]),
    ] + [
        pltpu.make_async_copy(w_hbm.at[pl.ds(first * 9, (3 - first) * 9), i], w_ref.at[i], in_sem.at[2 + i])
        for i in range(2)
    ]
    for load in loads:
        load.start()

    barrier = pltpu.get_barrier_semaphore()

    def greet(**where):
        pl.semaphore_signal(barrier, inc=1, device_id=where, device_id_type=MESH)

    peers = (1, 2) if quad else tuple(range(1, n_c))
    for k in peers:
        greet(chan=flip(chan, k, n_c))
    greet(rep=other)

    @pl.when(has_left)
    def _():
        greet(space=below)

    @pl.when(has_right)
    def _():
        greet(space=after)

    my_rows = pl.ds(pl.multiple_of(chan * in_part, in_part), in_part)
    loads[0].wait()
    for t in range(frames):
        for h in range(rows):
            v = x_ref[t, h].astype(F32)
            at = h * cols
            act[0, t, my_rows, at : at + cols] = (v * jax.nn.sigmoid(v)).astype(BF16)

    def shifts(row):
        v = row.astype(F32)
        lane = lax.broadcasted_iota(jnp.int32, v.shape, 1)
        ahead = jnp.where(lane < cols - 1, pltpu.roll(v, cols - 1, 1), 0.0)
        behind = jnp.where(lane > 0, pltpu.roll(v, 1, 1), 0.0)
        return ahead.astype(BF16), row, behind.astype(BF16)

    def lay_own(t, p, row):
        at = (t * (rows + 2) + p) * cols
        moved = shifts(row)
        for e in range(3):
            for i in range(2):
                gd[i, e * half : (e + 1) * half, at : at + cols] = moved[e][i * half : (i + 1) * half]

    def lay_sib(t, p, row):
        at = (t * (rows + 2) + p) * cols
        moved = shifts(row)
        for e in range(3):
            gs[e * half : (e + 1) * half, at : at + cols] = moved[e]

    loads[1].wait()
    for t in range(frames):
        for h in range(rows):
            lay_own(t, h + 1, g_ref[t, h])

    met = len(peers) + 1
    both = jnp.logical_and(has_left, has_right)

    @pl.when(both)
    def _():
        pl.semaphore_wait(barrier, met + 2)

    @pl.when(jnp.logical_not(both))
    def _():
        pl.semaphore_wait(barrier, met + (1 if n_s > 1 else 0))

    theirs = pl.ds(pl.multiple_of(other * half, half), half)

    def across(t):
        return remote(g_ref.at[t, :, theirs], sib_rows.at[t], c_send.at[t], c_recv.at[t], rep=other)

    def down(t):
        return remote(g_ref.at[t, rows - 1], halo.at[0, t], g_send.at[0, t], g_recv.at[0, t], space=after)

    def up(t):
        return remote(g_ref.at[t, 0], halo.at[1, t], g_send.at[1, t], g_recv.at[1, t], space=below)

    def down_sib(t):
        return remote(halo.at[0, t, theirs], sib_halo.at[0, t], g_send.at[2, t], g_recv.at[2, t], rep=other)

    def up_sib(t):
        return remote(halo.at[1, t, theirs], sib_halo.at[1, t], g_send.at[3, t], g_recv.at[3, t], rep=other)

    def chan_rows(k):
        owner = flip(chan, k, n_c)
        return pl.ds(pl.multiple_of(owner * in_part, in_part), in_part)

    def relay(k, t):
        return remote(act.at[0, t, chan_rows(k)], act.at[1, t, chan_rows(k)], b_send.at[k, t], b_recv.at[k, t], rep=other)

    def spread(k, t):
        return remote(act.at[0, t, my_rows], act.at[0, t, my_rows], a_send.at[k, t], a_recv.at[k, t], chan=flip(chan, k, n_c))

    def half_rows(k, i):
        span = in_part // 2
        return pl.ds(pl.multiple_of(flip(chan, k, n_c) * in_part + i * span, span), span)

    def pass_on(i, t):
        where = half_rows(1 + i, i)
        return remote(act.at[0, t, where], act.at[0, t, where], p_send.at[i, t], p_recv.at[i, t], chan=flip(chan, 2 - i, n_c))

    def pass_in(i, t):
        where = half_rows(3, i)
        return remote(act.at[0, t, where], act.at[0, t, where], p_send.at[i, t], p_recv.at[i, t], chan=flip(chan, 2 - i, n_c))

    for t in reversed(range(frames)):
        @pl.when(has_right)
        def _(t=t):
            down(t).start()

        @pl.when(has_left)
        def _(t=t):
            up(t).start()

    for t in range(frames):
        across(frames - 1 - t).start()
        relay(0, t).start()

    for t in range(frames):
        for k in peers:
            spread(k, t).start()

    def block_of(j):
        return flip(chan // per, j, blocks)

    def produce(n):
        j, k = order[n]
        a, b = pairs[k]
        where = pl.ds(pl.multiple_of(block_of(j) * width, width), width)
        value = None
        for t in range(frames):
            to = t + 2 - a
            if to < frames:
                at = to * deep + (2 - b) * cols
                term = nt(gd[rep, :, at : at + plane], act[0, t, where])
                term = term + nt(gs[:, at : at + plane], act[1, t, where])
                value = term if value is None else value + term
        for i in range(split):
            part[n * split + i] = value[i * piece : (i + 1) * piece]

    def own_edges(t):
        @pl.when(has_left)
        def _():
            down(t).wait_recv()
            down_sib(t).start()

        @pl.when(jnp.logical_not(has_left))
        def _():
            halo[0, t] = jnp.zeros_like(halo[0, t])
            sib_halo[0, t] = jnp.zeros_like(sib_halo[0, t])

        @pl.when(has_right)
        def _():
            up(t).wait_recv()
            up_sib(t).start()

        @pl.when(jnp.logical_not(has_right))
        def _():
            halo[1, t] = jnp.zeros_like(halo[1, t])
            sib_halo[1, t] = jnp.zeros_like(sib_halo[1, t])

        for i in range(2):
            lay_own(t, i * (rows + 1), halo[i, t])

    def sib_edges(t):
        @pl.when(has_left)
        def _():
            down_sib(t).wait_recv()

        @pl.when(has_right)
        def _():
            up_sib(t).wait_recv()

        for i in range(2):
            lay_sib(t, i * (rows + 1), sib_halo[i, t])

    def fetch(j, t):
        for k in range(j * per, (j + 1) * per):
            if quad and k == 3:
                pass_in(0, t).wait_recv()
                pass_in(1, t).wait_recv()
            elif k:
                spread(k, t).wait_recv()
            if k:
                relay(k, t).start()
            if quad and k in (1, 2):
                pass_on(k - 1, t).start()

    def settle(j, t):
        for k in range(j * per, (j + 1) * per):
            relay(k, t).wait_recv()

    middle = n_s // 2
    on_left = space < middle
    inner = jnp.where(on_left, space + 1, space - 1)
    outer = jnp.clip(jnp.where(on_left, space - 1, space + 1), 0, n_s - 1)
    depth = jnp.where(on_left, space, n_s - 1 - space)
    gap = jnp.where(on_left, middle - 1 - space, space - middle)
    central = gap == 0
    has_outer = depth > 0
    deepest = max(middle - 1, n_s - 1 - middle, 0)
    box = jnp.where(central, 1, 0)

    def send_sum(q):
        return remote(sums.at[q], inbox.at[box, q], s_send, s_recv.at[box, q], space=inner)

    def from_outer(q):
        return remote(sums.at[q], inbox.at[0, q], s_send, s_recv.at[0, q], space=inner)

    def from_peer(q):
        return remote(sums.at[q], inbox.at[1, q], s_send, s_recv.at[1, q], space=inner)

    def send_done(q):
        return remote(total.at[q], total.at[q], f_send, f_recv.at[q], space=outer)

    def keep(q):
        return pltpu.make_async_copy(total.at[q], total_hbm.at[q], out_sem.at[0])

    def live(q):
        return jnp.logical_and(q >= 0, q < pieces)

    def tick(time):
        sum_piece = time - LAG_SUM * depth
        done_piece = time - LAG_SUM * deepest - LAG_DONE * (1 + gap)

        @pl.when(live(sum_piece))
        def _():
            @pl.when(has_outer)
            def _():
                from_outer(sum_piece).wait_recv()
                sums[sum_piece] = (part[sum_piece] + inbox[0, sum_piece].astype(F32)).astype(BF16)

            @pl.when(jnp.logical_not(has_outer))
            def _():
                sums[sum_piece] = part[sum_piece].astype(BF16)

            if n_s > 1:
                send_sum(sum_piece).start()

        @pl.when(jnp.logical_and(jnp.logical_or(central, has_outer), live(done_piece)))
        def _():
            @pl.when(central)
            def _():
                value = sums[done_piece]
                if n_s > 1:
                    from_peer(done_piece).wait_recv()
                    value = (value.astype(F32) + inbox[1, done_piece].astype(F32)).astype(BF16)
                total[done_piece] = value

            @pl.when(jnp.logical_not(central))
            def _():
                send_done(done_piece).wait_recv()

            @pl.when(has_outer)
            def _():
                send_done(done_piece).start()

    def each(start, end, body):
        def run(i, carry):
            body(i)
            return carry

        lax.fori_loop(start, end, run, 0)

    def last(q):
        send_done(q).wait_recv()
        keep(q).start()

    calm = list(range(1, rows - 1))
    rim = [h for h in (0, rows - 1) if h not in calm]
    ranks = calm + rim[: 1 if rows == 1 else 2]

    def line_up(t, some):
        for b in range(3):
            for h in some:
                at = t * deep + (h + 2 - b) * cols
                to = ranks.index(h) * cols
                g3[t, b * 6 * half : (b + 1) * 6 * half, to : to + cols] = gd[:, :, at : at + cols].reshape(6 * half, cols)

    def input_grad(t, some):
        where = slice(ranks.index(some[0]) * cols, (ranks.index(some[-1]) + 1) * cols)
        value = None
        for a in range(first, 3):
            to = t + 2 - a
            if to < frames:
                term = nn(wt_ref[a - first], g3[to, :, where])
                value = term if value is None else value + term
        d_acc[t, :, where] = value
        d_out[t, :, where] = value.astype(BF16)

    def give(t, k):
        return remote(d_out.at[t, chan_rows(k)], d_one.at[t, k], d_send.at[t, k], d_recv.at[t, k], chan=flip(chan, k, n_c))

    def hop(t):
        return 1 + t % 2

    def give_one(t, k):
        block = hop(t) if k == 0 else 3
        return remote(
            d_out.at[t, chan_rows(block)], d_one.at[t, k], d_send.at[t, k], d_recv.at[t, k],
            chan=flip(chan, hop(t), n_c),
        )

    def give_two(t):
        return remote(d_mid.at[t], d_two.at[t], d_send.at[t, 2], d_recv.at[t, 2], chan=flip(chan, 3 - hop(t), n_c))

    def input_send(t):
        if quad:
            give_one(t, 1).start()
            give_one(t, 0).start()
        else:
            for k in peers:
                give(t, k).start()

    def input_mid(t):
        if quad:
            give_one(t, 1).wait_recv()
            d_mid[t] = (d_acc[t, chan_rows(3 - hop(t))] + d_one[t, 1].astype(F32)).astype(BF16)
            give_two(t).start()

    def input_end(t):
        if quad:
            give_one(t, 0).wait_recv()
            give_two(t).wait_recv()
        else:
            for k in peers:
                give(t, k).wait_recv()
        for h in range(rows):
            at = slice(ranks.index(h) * cols, (ranks.index(h) + 1) * cols)
            value = d_acc[t, my_rows, at]
            if quad:
                value = value + d_one[t, 0, :, at].astype(F32) + d_two[t, :, at].astype(F32)
            else:
                for k in peers:
                    value = value + d_one[t, k, :, at].astype(F32)
            v = x_ref[t, h].astype(F32)
            s = jax.nn.sigmoid(v)
            gi_ref[t, h] = (value * (s * (1.0 + v * (1.0 - s)))).astype(BF16)

    def input_sent(t):
        if quad:
            give_one(t, 0).wait_send()
            give_one(t, 1).wait_send()
            give_two(t).wait_send()
        else:
            for k in peers:
                give(t, k).wait_send()

    def inside(t):
        across(t).wait_recv()
        for h in range(rows):
            lay_sib(t, h + 1, sib_rows[t, h])

    def turn():
        loads[2].wait()
        loads[3].wait()
        for tap in range((3 - first) * 3):
            a, b = tap // 3, tap % 3
            wt_ref[a, :, b * 6 * half : (b + 1) * 6 * half] = w_ref[:, tap * 3 : tap * 3 + 3].reshape(6 * half, in_all).T

    before = {}
    turn()

    def at_unit(n, act_now):
        before.setdefault(n, []).append(act_now)

    def grad_part(some, send):
        if some:
            for t in range(frames):
                line_up(t, some)
            for t in reversed(range(frames)):
                input_grad(t, some)
        if send:
            for t in reversed(range(frames)):
                input_send(t)

    ends = jnp.logical_not(jnp.logical_or(central, has_outer))

    at_unit(0, functools.partial(inside, frames - 1))
    at_unit(0, functools.partial(settle, 0, 0))
    for t in range(1, frames):
        at_unit(1, functools.partial(inside, frames - 1 - t))
        at_unit(1, functools.partial(settle, 0, t))
    count = len(pairs)
    plain = 3 - first
    for t in reversed(range(1, frames)):
        at_unit(plain, functools.partial(own_edges, t))
    at_unit(plain, functools.partial(grad_part, calm, False))
    at_unit(plain, functools.partial(own_edges, 0))

    def inner_rim():
        pl.when(jnp.logical_not(ends))(functools.partial(grad_part, rim, True))

    def end_rim():
        pl.when(ends)(functools.partial(grad_part, rim, True))

    at_unit(plain, inner_rim)
    for t in reversed(range(1, frames)):
        at_unit(plain, functools.partial(sib_edges, t))
    at_unit(plain + 2 * (plain - 1), functools.partial(sib_edges, 0))
    at_unit(count - 1, end_rim)
    if quad:
        for t in range(frames):
            early = t < frames - 1
            for j in (1, 2):
                at_unit(count - 1 if early else count + 3, functools.partial(fetch, j, t))
            for j in (1, 2):
                at_unit(count if early else 2 * count, functools.partial(settle, j, t))
            at_unit(2 * count + 3, functools.partial(fetch, 3, t))
            at_unit(3 * count, functools.partial(settle, 3, t))
    else:
        for j in range(1, blocks):
            for t in range(frames):
                at_unit(j * count, functools.partial(fetch, j, t))
            for t in range(frames):
                at_unit(j * count, functools.partial(settle, j, t))
    for t in reversed(range(frames)):
        at_unit(units - 4, functools.partial(input_mid, t))

    for n in range(units):
        for act_now in before.get(n, []):
            act_now()
        produce(n)
        for i in range(split):
            tick(n * split + i)
    each(pieces, pieces + LAG_SUM * deepest + LAG_DONE * (1 + deepest), tick)
    for t in reversed(range(frames)):
        input_end(t)
    pltpu.make_async_copy(gi_ref, gi_hbm, out_sem.at[1]).start()

    @pl.when(ends)
    def _():
        each(0, pieces, last)

    @pl.when(jnp.logical_not(ends))
    def _():
        pltpu.make_async_copy(total, total_hbm, out_sem.at[0]).start()

    for t in range(frames):
        @pl.when(has_right)
        def _(t=t):
            down(t).wait_send()
            up_sib(t).wait_send()

        @pl.when(has_left)
        def _(t=t):
            up(t).wait_send()
            down_sib(t).wait_send()

        across(t).wait_send()
        for k in range(n_c):
            relay(k, t).wait_send()
        for k in peers:
            spread(k, t).wait_send()
        if quad:
            pass_on(0, t).wait_send()
            pass_on(1, t).wait_send()
        input_sent(t)
    if n_s > 1:
        remote(sums, inbox.at[0], s_send, s_recv.at[0, 0], space=inner).wait_send()

    @pl.when(has_outer)
    def _():
        remote(total, total, f_send, f_recv.at[0], space=outer).wait_send()

    pltpu.make_async_copy(total, total_hbm, out_sem.at[0]).wait()
    pltpu.make_async_copy(gi_ref, gi_hbm, out_sem.at[1]).wait()


def write(cfg, gi_in, total_hbm, gi_out, gw_out, gi_ref, total, stage, blank, in_sem, sem):
    n_c, n_s, frames, rows, in_part, out_part, cols, in_all = cfg
    half, width, blocks, per, chunk, split = sizes_of(cfg)
    pairs = taps_of(frames)
    order = order_of(cfg)
    first = max(0, 3 - frames)
    chan = lax.axis_index("chan")
    ranked = sorted(range(len(order)), key=lambda n: (order[n][1], n))
    loads = []
    for n in ranked:
        some = pl.ds(n * split, split)
        loads.append(pltpu.make_async_copy(total_hbm.at[some], total.at[some], in_sem.at[n]))
    loads.append(pltpu.make_async_copy(gi_in, gi_ref, in_sem.at[len(order)]))
    for load in loads:
        load.start()
    blank[...] = jnp.zeros_like(blank)
    copies = []
    for i in range(first * 3):
        copies.append(pltpu.make_async_copy(blank, gw_out.at[pl.ds(i * 3, 3)], sem.at[1 + i]))
        copies[-1].start()
    for i, n in enumerate(ranked):
        loads[i].wait()
        j, k = order[n]
        a, b = pairs[k]
        where = pl.ds(pl.multiple_of(flip(chan // per, j, blocks) * width, width), width)
        value = total[n * split : (n + 1) * split].astype(F32) * (1.0 / 256.0)
        stage[k, :, :, where] = value.reshape(3, half, width)
        if (i + 1) % blocks == 0:
            copies.append(pltpu.make_async_copy(stage.at[k], gw_out.at[pl.ds((a * 3 + b) * 3, 3)], sem.at[1 + a * 3 + b]))
            copies[-1].start()
    loads[-1].wait()
    copies.append(pltpu.make_async_copy(gi_ref, gi_out, sem.at[0]))
    copies[-1].start()
    for copy in copies:
        copy.wait()


def on_device(sizes, inputs, grad_out, weight):
    n_c, n_s = sizes
    _, frames, rows, in_part, cols = inputs.shape
    out_part = grad_out.shape[3]
    in_all = weight.shape[4]
    cfg = (n_c, n_s, frames, rows, in_part, out_part, cols, in_all)
    half, width, blocks, per, chunk, split = sizes_of(cfg)
    pairs = taps_of(frames)
    taps = len(pairs) * 3
    plane = rows * cols
    lanes = frames * (rows + 2) * cols
    units = blocks * len(pairs)
    slots = max(3, n_c)
    dma = pltpu.SemaphoreType.DMA
    pieces = units * split
    pile = (pieces, chunk // split, width)
    hbm = pl.BlockSpec(memory_space=pltpu.HBM)
    grad_in, total = pl.pallas_call(
        functools.partial(kernel, cfg),
        out_shape=(
            jax.ShapeDtypeStruct((frames, rows, in_part, cols), BF16),
            jax.ShapeDtypeStruct(pile, BF16),
        ),
        in_specs=[hbm, hbm, hbm],
        out_specs=(hbm, hbm),
        scratch_shapes=[
            pltpu.VMEM((frames, rows, in_part, cols), BF16),
            pltpu.VMEM(pile, BF16),
            pltpu.VMEM((frames, rows, in_part, cols), BF16),
            pltpu.VMEM((frames, rows, out_part, cols), BF16),
            pltpu.VMEM((2, taps, half, in_all), BF16),
            pltpu.VMEM((taps // 9, in_all, 18 * half), BF16),
            pltpu.VMEM((frames, 18 * half, plane), BF16),
            pltpu.VMEM((2, frames, in_all, plane), BF16),
            pltpu.VMEM((2, frames, out_part, cols), BF16),
            pltpu.VMEM((2, frames, half, cols), BF16),
            pltpu.VMEM((frames, rows, half, cols), BF16),
            pltpu.VMEM((2, 3 * half, lanes), BF16),
            pltpu.VMEM((3 * half, lanes), BF16),
            pltpu.VMEM(pile, F32),
            pltpu.VMEM(pile, BF16),
            pltpu.VMEM((2,) + pile, BF16),
            pltpu.VMEM((frames, in_all, plane), F32),
            pltpu.VMEM((frames, in_all, plane), BF16),
            pltpu.VMEM((frames, slots, in_part, plane), BF16),
            pltpu.VMEM((frames, in_part, plane), BF16),
            pltpu.VMEM((frames, in_part, plane), BF16),
            dma((4,)),
            dma((2,)),
            dma((4, frames)),
            dma((4, frames)),
            dma((frames,)),
            dma((frames,)),
            dma((n_c, frames)),
            dma((n_c, frames)),
            dma((2, frames)),
            dma((2, frames)),
            dma((n_c, frames)),
            dma((n_c, frames)),
            dma,
            dma((2, pieces)),
            dma,
            dma((pieces,)),
            dma((frames, slots)),
            dma((frames, slots)),
        ],
        compiler_params=pltpu.CompilerParams(
            collective_id=0, has_side_effects=True, vmem_limit_bytes=59 << 20
        ),
    )(
        inputs.reshape(frames, rows, in_part, cols),
        grad_out.reshape(frames, rows, out_part, cols),
        weight.reshape(27, 2, half, in_all),
    )
    grad_in, grad_weight = pl.pallas_call(
        functools.partial(write, cfg),
        out_shape=(
            jax.ShapeDtypeStruct((frames, rows, in_part, cols), BF16),
            jax.ShapeDtypeStruct((27, half, in_all), F32),
        ),
        in_specs=[hbm, hbm],
        out_specs=(hbm, hbm),
        scratch_shapes=[
            pltpu.VMEM((frames, rows, in_part, cols), BF16),
            pltpu.VMEM(pile, BF16),
            pltpu.VMEM((len(pairs), 3, half, in_all), F32),
            pltpu.VMEM((3, half, in_all), F32),
            dma((units + 1,)),
            dma((10,)),
        ],
        compiler_params=pltpu.CompilerParams(vmem_limit_bytes=59 << 20),
    )(grad_in, total)
    return grad_in.reshape(inputs.shape), grad_weight.reshape(3, 3, 3, half, in_all)


def solution(mesh):
    return jax.shard_map(
        functools.partial(on_device, (mesh.shape["chan"], mesh.shape["space"])),
        mesh=mesh,
        in_specs=(
            P("rep", None, "space", "chan", None),
            P("rep", None, "space", "chan", None),
            P(None, None, None, "chan", None),
        ),
        out_specs=(
            P("rep", None, "space", "chan", None),
            P(None, None, None, ("chan", "rep"), None),
        ),
        check_vma=False,
    )
```

```python
import functools

import jax
import jax.numpy as jnp
from jax import lax
from jax.experimental import pallas as pl
from jax.experimental.pallas import tpu as pltpu
from jax.sharding import PartitionSpec as P

MESH = pl.DeviceIdType.MESH
F32 = jnp.float32
BF16 = jnp.bfloat16
LANES = 128
LAG_SUM = 5
LAG_DONE = 7


def flip(index, mask, count):
    out, bit = 0, 1
    while bit < count:
        out = out + (((index // bit) + ((mask // bit) % 2)) % 2) * bit
        bit *= 2
    return out


def nt(a, b):
    return lax.dot_general(a, b, (((1,), (1,)), ((), ())), preferred_element_type=F32)


def nn(a, b):
    return lax.dot_general(a, b, (((1,), (0,)), ((), ())), preferred_element_type=F32)


def taps_of(frames):
    taps = range(max(0, 3 - frames), 3)
    return [(a, 1) for a in taps] + [(a, b) for a in taps for b in (0, 2)]


def sizes_of(cfg):
    n_c, n_s, frames, rows, in_part, out_part, cols, in_all = cfg
    half = out_part // 2
    width = max(LANES, in_part)
    blocks = in_all // width
    chunk = 3 * half
    split = 2 if chunk % 32 == 0 else 1
    return half, width, blocks, width // in_part, chunk, split


def order_of(cfg):
    half, width, blocks, per, chunk, split = sizes_of(cfg)
    pairs = taps_of(cfg[2])
    every = range(len(pairs))
    if cfg[0] != 4:
        return [(j, k) for j in range(blocks) for k in every]
    low = [k for k in every if pairs[k][0] < 2]
    high = [k for k in every if pairs[k][0] == 2]
    order = [(0, k) for k in every]
    for group in ((1, 2), (3,)):
        for part in (low, high):
            order += [(j, k) for j in group for k in part]
    return order


def kernel(
    cfg,
    xg_ref, w_hbm,
    gi_ref, total,
    w_ref, wt_ref, g3, act, halo, sib_halo, sib_rows, gd, gs,
    part, sums, inbox, d_acc, d_out, d_one, d_two, d_mid,
    in_sem, g_send, g_recv, c_send, c_recv, a_send, a_recv, p_send, p_recv, b_send, b_recv,
    s_send, s_recv, f_send, f_recv, d_send, d_recv,
):
    n_c, n_s, frames, rows, in_part, out_part, cols, in_all = cfg
    half, width, blocks, per, chunk, split = sizes_of(cfg)
    pairs = taps_of(frames)
    order = order_of(cfg)
    first = max(0, 3 - frames)
    plane = rows * cols
    deep = (rows + 2) * cols
    units = len(order)
    pieces = units * split
    piece = chunk // split
    quad = n_c == 4

    x_ref, g_ref = xg_ref.at[0], xg_ref.at[1]
    chan = lax.axis_index("chan")
    space = lax.axis_index("space")
    rep = lax.axis_index("rep")
    other = 1 - rep
    has_left = space > 0
    has_right = space < n_s - 1
    after = (space + 1) % n_s
    below = (space + n_s - 1) % n_s

    def remote(src, dst, ssem, rsem, **where):
        return pltpu.make_async_remote_copy(
            src_ref=src, dst_ref=dst, send_sem=ssem, recv_sem=rsem,
            device_id=where, device_id_type=MESH,
        )

    loads = [
        None, None,
    ] + [
        pltpu.make_async_copy(w_hbm.at[pl.ds(first * 9, (3 - first) * 9), i], w_ref.at[i], in_sem.at[2 + i])
        for i in range(2)
    ]
    for load in loads[2:]:
        load.start()

    barrier = pltpu.get_barrier_semaphore()

    def greet(**where):
        pl.semaphore_signal(barrier, inc=1, device_id=where, device_id_type=MESH)

    peers = (1, 2) if quad else tuple(range(1, n_c))
    for k in peers:
        greet(chan=flip(chan, k, n_c))
    greet(rep=other)

    @pl.when(has_left)
    def _():
        greet(space=below)

    @pl.when(has_right)
    def _():
        greet(space=after)

    my_rows = pl.ds(pl.multiple_of(chan * in_part, in_part), in_part)
    for t in range(frames):
        for h in range(rows):
            v = x_ref[t, h].astype(F32)
            at = h * cols
            act[0, t, my_rows, at : at + cols] = (v * jax.nn.sigmoid(v)).astype(BF16)

    def shifts(row):
        v = row.astype(F32)
        lane = lax.broadcasted_iota(jnp.int32, v.shape, 1)
        ahead = jnp.where(lane < cols - 1, pltpu.roll(v, cols - 1, 1), 0.0)
        behind = jnp.where(lane > 0, pltpu.roll(v, 1, 1), 0.0)
        return ahead.astype(BF16), row, behind.astype(BF16)

    def lay_own(t, p, row):
        at = (t * (rows + 2) + p) * cols
        moved = shifts(row)
        for e in range(3):
            for i in range(2):
                gd[i, e * half : (e + 1) * half, at : at + cols] = moved[e][i * half : (i + 1) * half]

    def lay_sib(t, p, row):
        at = (t * (rows + 2) + p) * cols
        moved = shifts(row)
        for e in range(3):
            gs[e * half : (e + 1) * half, at : at + cols] = moved[e]

    met = len(peers) + 1
    both = jnp.logical_and(has_left, has_right)

    @pl.when(both)
    def _():
        pl.semaphore_wait(barrier, met + 2)

    @pl.when(jnp.logical_not(both))
    def _():
        pl.semaphore_wait(barrier, met + (1 if n_s > 1 else 0))

    theirs = pl.ds(pl.multiple_of(other * half, half), half)

    def across(t):
        return remote(g_ref.at[t, :, theirs], sib_rows.at[t], c_send.at[t], c_recv.at[t], rep=other)

    def down(t):
        return remote(g_ref.at[t, rows - 1], halo.at[0, t], g_send.at[0, t], g_recv.at[0, t], space=after)

    def up(t):
        return remote(g_ref.at[t, 0], halo.at[1, t], g_send.at[1, t], g_recv.at[1, t], space=below)

    def down_sib(t):
        return remote(halo.at[0, t, theirs], sib_halo.at[0, t], g_send.at[2, t], g_recv.at[2, t], rep=other)

    def up_sib(t):
        return remote(halo.at[1, t, theirs], sib_halo.at[1, t], g_send.at[3, t], g_recv.at[3, t], rep=other)

    def chan_rows(k):
        owner = flip(chan, k, n_c)
        return pl.ds(pl.multiple_of(owner * in_part, in_part), in_part)

    def relay(k, t):
        return remote(act.at[0, t, chan_rows(k)], act.at[1, t, chan_rows(k)], b_send.at[k, t], b_recv.at[k, t], rep=other)

    def spread(k, t):
        return remote(act.at[0, t, my_rows], act.at[0, t, my_rows], a_send.at[k, t], a_recv.at[k, t], chan=flip(chan, k, n_c))

    def half_rows(k, i):
        span = in_part // 2
        return pl.ds(pl.multiple_of(flip(chan, k, n_c) * in_part + i * span, span), span)

    def pass_on(i, t):
        where = half_rows(1 + i, i)
        return remote(act.at[0, t, where], act.at[0, t, where], p_send.at[i, t], p_recv.at[i, t], chan=flip(chan, 2 - i, n_c))

    def pass_in(i, t):
        where = half_rows(3, i)
        return remote(act.at[0, t, where], act.at[0, t, where], p_send.at[i, t], p_recv.at[i, t], chan=flip(chan, 2 - i, n_c))

    for t in reversed(range(frames)):
        @pl.when(has_right)
        def _(t=t):
            down(t).start()

        @pl.when(has_left)
        def _(t=t):
            up(t).start()

    for t in range(frames):
        across(frames - 1 - t).start()
        relay(0, t).start()

    for t in range(frames):
        for k in peers:
            spread(k, t).start()

    for t in range(frames):
        for h in range(rows):
            lay_own(t, h + 1, g_ref[t, h])

    def block_of(j):
        return flip(chan // per, j, blocks)

    def produce(n):
        j, k = order[n]
        a, b = pairs[k]
        where = pl.ds(pl.multiple_of(block_of(j) * width, width), width)
        value = None
        for t in range(frames):
            to = t + 2 - a
            if to < frames:
                at = to * deep + (2 - b) * cols
                term = nt(gd[rep, :, at : at + plane], act[0, t, where])
                term = term + nt(gs[:, at : at + plane], act[1, t, where])
                value = term if value is None else value + term
        for i in range(split):
            part[n * split + i] = value[i * piece : (i + 1) * piece]

    def own_edges(t):
        @pl.when(has_left)
        def _():
            down(t).wait_recv()
            down_sib(t).start()

        @pl.when(jnp.logical_not(has_left))
        def _():
            halo[0, t] = jnp.zeros_like(halo[0, t])
            sib_halo[0, t] = jnp.zeros_like(sib_halo[0, t])

        @pl.when(has_right)
        def _():
            up(t).wait_recv()
            up_sib(t).start()

        @pl.when(jnp.logical_not(has_right))
        def _():
            halo[1, t] = jnp.zeros_like(halo[1, t])
            sib_halo[1, t] = jnp.zeros_like(sib_halo[1, t])

        for i in range(2):
            lay_own(t, i * (rows + 1), halo[i, t])

    def sib_edges(t):
        @pl.when(has_left)
        def _():
            down_sib(t).wait_recv()

        @pl.when(has_right)
        def _():
            up_sib(t).wait_recv()

        for i in range(2):
            lay_sib(t, i * (rows + 1), sib_halo[i, t])

    def fetch(j, t):
        for k in range(j * per, (j + 1) * per):
            if quad and k == 3:
                pass_in(0, t).wait_recv()
                pass_in(1, t).wait_recv()
            elif k:
                spread(k, t).wait_recv()
            if k:
                relay(k, t).start()
            if quad and k in (1, 2):
                pass_on(k - 1, t).start()

    def settle(j, t):
        for k in range(j * per, (j + 1) * per):
            relay(k, t).wait_recv()

    middle = n_s // 2
    on_left = space < middle
    inner = jnp.where(on_left, space + 1, space - 1)
    outer = jnp.clip(jnp.where(on_left, space - 1, space + 1), 0, n_s - 1)
    depth = jnp.where(on_left, space, n_s - 1 - space)
    gap = jnp.where(on_left, middle - 1 - space, space - middle)
    central = gap == 0
    has_outer = depth > 0
    deepest = max(middle - 1, n_s - 1 - middle, 0)
    box = jnp.where(central, 1, 0)

    def send_sum(q):
        return remote(sums.at[q], inbox.at[box, q], s_send, s_recv.at[box, q], space=inner)

    def from_outer(q):
        return remote(sums.at[q], inbox.at[0, q], s_send, s_recv.at[0, q], space=inner)

    def from_peer(q):
        return remote(sums.at[q], inbox.at[1, q], s_send, s_recv.at[1, q], space=inner)

    def send_done(q):
        return remote(total.at[q], total.at[q], f_send, f_recv.at[q], space=outer)


    def live(q):
        return jnp.logical_and(q >= 0, q < pieces)

    def tick(time):
        sum_piece = time - LAG_SUM * depth
        done_piece = time - LAG_SUM * deepest - LAG_DONE * (1 + gap)

        @pl.when(live(sum_piece))
        def _():
            @pl.when(has_outer)
            def _():
                from_outer(sum_piece).wait_recv()
                sums[sum_piece] = (part[sum_piece] + inbox[0, sum_piece].astype(F32)).astype(BF16)

            @pl.when(jnp.logical_not(has_outer))
            def _():
                sums[sum_piece] = part[sum_piece].astype(BF16)

            if n_s > 1:
                send_sum(sum_piece).start()

        @pl.when(jnp.logical_and(jnp.logical_or(central, has_outer), live(done_piece)))
        def _():
            @pl.when(central)
            def _():
                value = sums[done_piece]
                if n_s > 1:
                    from_peer(done_piece).wait_recv()
                    value = (value.astype(F32) + inbox[1, done_piece].astype(F32)).astype(BF16)
                total[done_piece] = value

            @pl.when(jnp.logical_not(central))
            def _():
                send_done(done_piece).wait_recv()

            @pl.when(has_outer)
            def _():
                send_done(done_piece).start()

    four = n_s == 4

    def near(q):
        sums[q] = part[q].astype(BF16)
        from_outer(q).start()

    def relayed(q):
        if 0 <= q < pieces:
            from_outer(q).wait_recv()
            sums[q] = (part[q] + inbox[0, q].astype(F32)).astype(BF16)
            from_peer(q).start()
        q = q - LAG_DONE
        if 0 <= q < pieces:
            from_peer(q).wait_recv()
            total[q] = (sums[q].astype(F32) + inbox[1, q].astype(F32)).astype(BF16)
            send_done(q).start()

    def ticks(start, end):
        if not four:
            for time in range(start, end):
                tick(time)
            return

        @pl.when(central)
        def _():
            for time in range(start, end):
                relayed(time - LAG_SUM)

        if start < pieces:
            @pl.when(jnp.logical_not(central))
            def _():
                for time in range(start, min(end, pieces)):
                    near(time)

    def each(start, end, body):
        def run(i, carry):
            body(i)
            return carry

        lax.fori_loop(start, end, run, 0)

    def last(q):
        send_done(q).wait_recv()

    calm = list(range(1, rows - 1))
    rim = [h for h in (0, rows - 1) if h not in calm]
    ranks = calm + rim[: 1 if rows == 1 else 2]

    def line_up(t, some):
        for b in range(3):
            for h in some:
                at = t * deep + (h + 2 - b) * cols
                to = ranks.index(h) * cols
                g3[t, b * 6 * half : (b + 1) * 6 * half, to : to + cols] = gd[:, :, at : at + cols].reshape(6 * half, cols)

    def input_grad(t, some):
        where = slice(ranks.index(some[0]) * cols, (ranks.index(some[-1]) + 1) * cols)
        value = None
        for a in range(first, 3):
            to = t + 2 - a
            if to < frames:
                term = nn(wt_ref[a - first], g3[to, :, where])
                value = term if value is None else value + term
        d_acc[t, :, where] = value
        d_out[t, :, where] = value.astype(BF16)

    def give(t, k):
        return remote(d_out.at[t, chan_rows(k)], d_one.at[t, k], d_send.at[t, k], d_recv.at[t, k], chan=flip(chan, k, n_c))

    def hop(t):
        return 1 + t % 2

    def give_one(t, k):
        block = hop(t) if k == 0 else 3
        return remote(
            d_out.at[t, chan_rows(block)], d_one.at[t, k], d_send.at[t, k], d_recv.at[t, k],
            chan=flip(chan, hop(t), n_c),
        )

    def give_two(t):
        return remote(d_mid.at[t], d_two.at[t], d_send.at[t, 2], d_recv.at[t, 2], chan=flip(chan, 3 - hop(t), n_c))

    def input_send(t):
        if quad:
            give_one(t, 1).start()
            give_one(t, 0).start()
        else:
            for k in peers:
                give(t, k).start()

    def input_mid(t):
        if quad:
            give_one(t, 1).wait_recv()
            d_mid[t] = (d_acc[t, chan_rows(3 - hop(t))] + d_one[t, 1].astype(F32)).astype(BF16)
            give_two(t).start()

    def input_end(t):
        if quad:
            give_one(t, 0).wait_recv()
            give_two(t).wait_recv()
        else:
            for k in peers:
                give(t, k).wait_recv()
        for h in range(rows):
            at = slice(ranks.index(h) * cols, (ranks.index(h) + 1) * cols)
            value = d_acc[t, my_rows, at]
            if quad:
                value = value + d_one[t, 0, :, at].astype(F32) + d_two[t, :, at].astype(F32)
            else:
                for k in peers:
                    value = value + d_one[t, k, :, at].astype(F32)
            v = x_ref[t, h].astype(F32)
            s = jax.nn.sigmoid(v)
            gi_ref[t, h] = (value * (s * (1.0 + v * (1.0 - s)))).astype(BF16)

    def input_sent(t):
        if quad:
            give_one(t, 0).wait_send()
            give_one(t, 1).wait_send()
            give_two(t).wait_send()
        else:
            for k in peers:
                give(t, k).wait_send()

    def inside(t):
        across(t).wait_recv()
        for h in range(rows):
            lay_sib(t, h + 1, sib_rows[t, h])

    def turn():
        loads[2].wait()
        loads[3].wait()
        for tap in range((3 - first) * 3):
            a, b = tap // 3, tap % 3
            wt_ref[a, :, b * 6 * half : (b + 1) * 6 * half] = w_ref[:, tap * 3 : tap * 3 + 3].reshape(6 * half, in_all).T

    before = {}
    turn()

    def at_unit(n, act_now):
        before.setdefault(n, []).append(act_now)

    def grad_part(some, send):
        if some:
            for t in range(frames):
                line_up(t, some)
            for t in reversed(range(frames)):
                input_grad(t, some)
        if send:
            for t in reversed(range(frames)):
                input_send(t)

    ends = jnp.logical_not(jnp.logical_or(central, has_outer))

    at_unit(0, functools.partial(inside, frames - 1))
    at_unit(0, functools.partial(settle, 0, 0))
    for t in range(1, frames):
        at_unit(1, functools.partial(inside, frames - 1 - t))
        at_unit(1, functools.partial(settle, 0, t))
    count = len(pairs)
    plain = 3 - first
    for t in reversed(range(1, frames)):
        at_unit(plain, functools.partial(own_edges, t))
    at_unit(plain, functools.partial(grad_part, calm, False))
    at_unit(plain, functools.partial(own_edges, 0))

    def inner_rim():
        pl.when(jnp.logical_not(ends))(functools.partial(grad_part, rim, True))

    def end_rim():
        pl.when(ends)(functools.partial(grad_part, rim, True))

    at_unit(plain, inner_rim)
    for t in reversed(range(1, frames)):
        at_unit(plain, functools.partial(sib_edges, t))
    at_unit(plain + 2 * (plain - 1), functools.partial(sib_edges, 0))
    at_unit(count - 1, end_rim)
    if quad:
        for t in range(frames):
            early = t < frames - 1
            for j in (1, 2):
                at_unit(count - 1 if early else count + 3, functools.partial(fetch, j, t))
            for j in (1, 2):
                at_unit(count if early else 2 * count, functools.partial(settle, j, t))
            at_unit(2 * count + 3, functools.partial(fetch, 3, t))
            at_unit(3 * count, functools.partial(settle, 3, t))
    else:
        for j in range(1, blocks):
            for t in range(frames):
                at_unit(j * count, functools.partial(fetch, j, t))
            for t in range(frames):
                at_unit(j * count, functools.partial(settle, j, t))
    for t in reversed(range(frames)):
        at_unit(units - 4, functools.partial(input_mid, t))

    for n in range(units):
        for act_now in before.get(n, []):
            act_now()
        produce(n)
        ticks(n * split, (n + 1) * split)
    if four:
        ticks(pieces, pieces + LAG_SUM + LAG_DONE)
    else:
        each(pieces, pieces + LAG_SUM * deepest + LAG_DONE * (1 + deepest), tick)
    for t in reversed(range(frames)):
        input_end(t)

    @pl.when(ends)
    def _():
        each(0, pieces, last)


    for t in range(frames):
        @pl.when(has_right)
        def _(t=t):
            down(t).wait_send()
            up_sib(t).wait_send()

        @pl.when(has_left)
        def _(t=t):
            up(t).wait_send()
            down_sib(t).wait_send()

        across(t).wait_send()
        for k in range(n_c):
            relay(k, t).wait_send()
        for k in peers:
            spread(k, t).wait_send()
        if quad:
            pass_on(0, t).wait_send()
            pass_on(1, t).wait_send()
        input_sent(t)
    if n_s > 1:
        remote(sums, inbox.at[0], s_send, s_recv.at[0, 0], space=inner).wait_send()

    @pl.when(has_outer)
    def _():
        remote(total, total, f_send, f_recv.at[0], space=outer).wait_send()


def write(cfg, gi_ref, total, gi_out, gw_out, stage, blank, sem):
    n_c, n_s, frames, rows, in_part, out_part, cols, in_all = cfg
    half, width, blocks, per, chunk, split = sizes_of(cfg)
    pairs = taps_of(frames)
    order = order_of(cfg)
    first = max(0, 3 - frames)
    chan = lax.axis_index("chan")
    ranked = sorted(range(len(order)), key=lambda n: (order[n][1], n))
    blank[...] = jnp.zeros_like(blank)
    copies = []
    for i in range(first * 3):
        copies.append(pltpu.make_async_copy(blank, gw_out.at[pl.ds(i * 3, 3)], sem.at[1 + i]))
        copies[-1].start()
    for i, n in enumerate(ranked):
        j, k = order[n]
        a, b = pairs[k]
        where = pl.ds(pl.multiple_of(flip(chan // per, j, blocks) * width, width), width)
        value = total[n * split : (n + 1) * split].astype(F32) * (1.0 / 256.0)
        stage[k, :, :, where] = value.reshape(3, half, width)
        if (i + 1) % blocks == 0:
            copies.append(pltpu.make_async_copy(stage.at[k], gw_out.at[pl.ds((a * 3 + b) * 3, 3)], sem.at[1 + a * 3 + b]))
            copies[-1].start()
    copies.append(pltpu.make_async_copy(gi_ref, gi_out, sem.at[0]))
    copies[-1].start()
    for copy in copies:
        copy.wait()


def on_device(sizes, inputs, grad_out, weight):
    n_c, n_s = sizes
    _, frames, rows, in_part, cols = inputs.shape
    out_part = grad_out.shape[3]
    in_all = weight.shape[4]
    cfg = (n_c, n_s, frames, rows, in_part, out_part, cols, in_all)
    half, width, blocks, per, chunk, split = sizes_of(cfg)
    pairs = taps_of(frames)
    taps = len(pairs) * 3
    plane = rows * cols
    lanes = frames * (rows + 2) * cols
    units = blocks * len(pairs)
    slots = max(3, n_c)
    dma = pltpu.SemaphoreType.DMA
    pieces = units * split
    pile = (pieces, chunk // split, width)
    vmem = pl.BlockSpec(memory_space=pltpu.VMEM)
    hbm = pl.BlockSpec(memory_space=pltpu.HBM)
    grad_in, total = pl.pallas_call(
        functools.partial(kernel, cfg),
        out_shape=(
            jax.ShapeDtypeStruct((frames, rows, in_part, cols), BF16),
            jax.ShapeDtypeStruct(pile, BF16),
        ),
        in_specs=[vmem, hbm],
        out_specs=(vmem, vmem),
        scratch_shapes=[
            pltpu.VMEM((2, taps, half, in_all), BF16),
            pltpu.VMEM((taps // 9, in_all, 18 * half), BF16),
            pltpu.VMEM((frames, 18 * half, plane), BF16),
            pltpu.VMEM((2, frames, in_all, plane), BF16),
            pltpu.VMEM((2, frames, out_part, cols), BF16),
            pltpu.VMEM((2, frames, half, cols), BF16),
            pltpu.VMEM((frames, rows, half, cols), BF16),
            pltpu.VMEM((2, 3 * half, lanes), BF16),
            pltpu.VMEM((3 * half, lanes), BF16),
            pltpu.VMEM(pile, F32),
            pltpu.VMEM(pile, BF16),
            pltpu.VMEM((2,) + pile, BF16),
            pltpu.VMEM((frames, in_all, plane), F32),
            pltpu.VMEM((frames, in_all, plane), BF16),
            pltpu.VMEM((frames, slots, in_part, plane), BF16),
            pltpu.VMEM((frames, in_part, plane), BF16),
            pltpu.VMEM((frames, in_part, plane), BF16),
            dma((4,)),
            dma((4, frames)),
            dma((4, frames)),
            dma((frames,)),
            dma((frames,)),
            dma((n_c, frames)),
            dma((n_c, frames)),
            dma((2, frames)),
            dma((2, frames)),
            dma((n_c, frames)),
            dma((n_c, frames)),
            dma,
            dma((2, pieces)),
            dma,
            dma((pieces,)),
            dma((frames, slots)),
            dma((frames, slots)),
        ],
        compiler_params=pltpu.CompilerParams(
            collective_id=0, has_side_effects=True, vmem_limit_bytes=50 << 20
        ),
    )(
        jnp.stack([inputs.reshape(frames, rows, in_part, cols), grad_out.reshape(frames, rows, out_part, cols)]),
        weight.reshape(27, 2, half, in_all),
    )
    grad_in, grad_weight = pl.pallas_call(
        functools.partial(write, cfg),
        out_shape=(
            jax.ShapeDtypeStruct((frames, rows, in_part, cols), BF16),
            jax.ShapeDtypeStruct((27, half, in_all), F32),
        ),
        in_specs=[vmem, vmem],
        out_specs=(hbm, hbm),
        scratch_shapes=[
            pltpu.VMEM((len(pairs), 3, half, in_all), F32),
            pltpu.VMEM((3, half, in_all), F32),
            dma((10,)),
        ],
        compiler_params=pltpu.CompilerParams(vmem_limit_bytes=50 << 20),
    )(grad_in, total)
    return grad_in.reshape(inputs.shape), grad_weight.reshape(3, 3, 3, half, in_all)


def solution(mesh):
    return jax.shard_map(
        functools.partial(on_device, (mesh.shape["chan"], mesh.shape["space"])),
        mesh=mesh,
        in_specs=(
            P("rep", None, "space", "chan", None),
            P("rep", None, "space", "chan", None),
            P(None, None, None, "chan", None),
        ),
        out_specs=(
            P("rep", None, "space", "chan", None),
            P(None, None, None, ("chan", "rep"), None),
        ),
        check_vma=False,
    )
```

```python
import functools

import jax
import jax.numpy as jnp
from jax import lax
from jax.experimental import pallas as pl
from jax.experimental.pallas import tpu as pltpu
from jax.sharding import PartitionSpec as P

MESH = pl.DeviceIdType.MESH
F32 = jnp.float32
BF16 = jnp.bfloat16
LANES = 128
LAG_SUM = 5
LAG_DONE = 6


def flip(index, mask, count):
    out, bit = 0, 1
    while bit < count:
        out = out + (((index // bit) + ((mask // bit) % 2)) % 2) * bit
        bit *= 2
    return out


def nt(a, b):
    return lax.dot_general(a, b, (((1,), (1,)), ((), ())), preferred_element_type=F32)


def nn(a, b):
    return lax.dot_general(a, b, (((1,), (0,)), ((), ())), preferred_element_type=F32)


def taps_of(frames):
    taps = range(max(0, 3 - frames), 3)
    return [(a, 1) for a in taps] + [(a, b) for a in taps for b in (0, 2)]


def sizes_of(cfg):
    n_c, n_s, frames, rows, in_part, out_part, cols, in_all = cfg
    half = out_part // 2
    width = max(LANES, in_part)
    blocks = in_all // width
    chunk = 3 * half
    split = 2 if chunk % 32 == 0 else 1
    return half, width, blocks, width // in_part, chunk, split


def order_of(cfg):
    half, width, blocks, per, chunk, split = sizes_of(cfg)
    pairs = taps_of(cfg[2])
    every = range(len(pairs))
    if cfg[0] != 4:
        return [(j, k) for j in range(blocks) for k in every]
    low = [k for k in every if pairs[k][0] < 2]
    high = [k for k in every if pairs[k][0] == 2]
    order = [(0, k) for k in every]
    for group in ((1, 2), (3,)):
        for part in (low, high):
            order += [(j, k) for j in group for k in part]
    return order


def kernel(
    cfg,
    xg_ref, w_hbm,
    gi_ref, total,
    w_ref, wt_ref, g3, act, halo, sib_halo, sib_rows, gd, gs,
    part, sums, inbox, d_acc, d_out, d_one, d_two, d_mid,
    in_sem, g_send, g_recv, c_send, c_recv, a_send, a_recv, p_send, p_recv, b_send, b_recv,
    s_send, s_recv, f_send, f_recv, d_send, d_recv,
):
    n_c, n_s, frames, rows, in_part, out_part, cols, in_all = cfg
    half, width, blocks, per, chunk, split = sizes_of(cfg)
    pairs = taps_of(frames)
    order = order_of(cfg)
    first = max(0, 3 - frames)
    plane = rows * cols
    deep = (rows + 2) * cols
    units = len(order)
    pieces = units * split
    piece = chunk // split
    quad = n_c == 4

    x_ref, g_ref = xg_ref.at[0], xg_ref.at[1]
    chan = lax.axis_index("chan")
    space = lax.axis_index("space")
    rep = lax.axis_index("rep")
    other = 1 - rep
    has_left = space > 0
    has_right = space < n_s - 1
    after = (space + 1) % n_s
    below = (space + n_s - 1) % n_s

    def remote(src, dst, ssem, rsem, **where):
        return pltpu.make_async_remote_copy(
            src_ref=src, dst_ref=dst, send_sem=ssem, recv_sem=rsem,
            device_id=where, device_id_type=MESH,
        )

    loads = [
        None, None,
    ] + [
        pltpu.make_async_copy(w_hbm.at[pl.ds(first * 9, (3 - first) * 9), i], w_ref.at[i], in_sem.at[2 + i])
        for i in range(2)
    ]
    for load in loads[2:]:
        load.start()

    barrier = pltpu.get_barrier_semaphore()

    def greet(**where):
        pl.semaphore_signal(barrier, inc=1, device_id=where, device_id_type=MESH)

    peers = (1, 2) if quad else tuple(range(1, n_c))
    for k in peers:
        greet(chan=flip(chan, k, n_c))
    greet(rep=other)

    @pl.when(has_left)
    def _():
        greet(space=below)

    @pl.when(has_right)
    def _():
        greet(space=after)

    my_rows = pl.ds(pl.multiple_of(chan * in_part, in_part), in_part)
    for t in range(frames):
        for h in range(rows):
            v = x_ref[t, h].astype(F32)
            at = h * cols
            act[0, t, my_rows, at : at + cols] = (v * jax.nn.sigmoid(v)).astype(BF16)

    def shifts(row):
        v = row.astype(F32)
        lane = lax.broadcasted_iota(jnp.int32, v.shape, 1)
        ahead = jnp.where(lane < cols - 1, pltpu.roll(v, cols - 1, 1), 0.0)
        behind = jnp.where(lane > 0, pltpu.roll(v, 1, 1), 0.0)
        return ahead.astype(BF16), row, behind.astype(BF16)

    def lay_own(t, p, row):
        at = (t * (rows + 2) + p) * cols
        moved = shifts(row)
        for e in range(3):
            for i in range(2):
                gd[i, e * half : (e + 1) * half, at : at + cols] = moved[e][i * half : (i + 1) * half]

    def lay_sib(t, p, row):
        at = (t * (rows + 2) + p) * cols
        moved = shifts(row)
        for e in range(3):
            gs[e * half : (e + 1) * half, at : at + cols] = moved[e]

    met = len(peers) + 1
    both = jnp.logical_and(has_left, has_right)

    @pl.when(both)
    def _():
        pl.semaphore_wait(barrier, met + 2)

    @pl.when(jnp.logical_not(both))
    def _():
        pl.semaphore_wait(barrier, met + (1 if n_s > 1 else 0))

    theirs = pl.ds(pl.multiple_of(other * half, half), half)

    def across(t):
        return remote(g_ref.at[t, :, theirs], sib_rows.at[t], c_send.at[t], c_recv.at[t], rep=other)

    def down(t):
        return remote(g_ref.at[t, rows - 1], halo.at[0, t], g_send.at[0, t], g_recv.at[0, t], space=after)

    def up(t):
        return remote(g_ref.at[t, 0], halo.at[1, t], g_send.at[1, t], g_recv.at[1, t], space=below)

    def down_sib(t):
        return remote(halo.at[0, t, theirs], sib_halo.at[0, t], g_send.at[2, t], g_recv.at[2, t], rep=other)

    def up_sib(t):
        return remote(halo.at[1, t, theirs], sib_halo.at[1, t], g_send.at[3, t], g_recv.at[3, t], rep=other)

    def chan_rows(k):
        owner = flip(chan, k, n_c)
        return pl.ds(pl.multiple_of(owner * in_part, in_part), in_part)

    def relay(k, t):
        return remote(act.at[0, t, chan_rows(k)], act.at[1, t, chan_rows(k)], b_send.at[k, t], b_recv.at[k, t], rep=other)

    def spread(k, t):
        return remote(act.at[0, t, my_rows], act.at[0, t, my_rows], a_send.at[k, t], a_recv.at[k, t], chan=flip(chan, k, n_c))

    def half_rows(k, i):
        span = in_part // 2
        return pl.ds(pl.multiple_of(flip(chan, k, n_c) * in_part + i * span, span), span)

    def pass_on(i, t):
        where = half_rows(1 + i, i)
        return remote(act.at[0, t, where], act.at[0, t, where], p_send.at[i, t], p_recv.at[i, t], chan=flip(chan, 2 - i, n_c))

    def pass_in(i, t):
        where = half_rows(3, i)
        return remote(act.at[0, t, where], act.at[0, t, where], p_send.at[i, t], p_recv.at[i, t], chan=flip(chan, 2 - i, n_c))

    for t in reversed(range(frames)):
        @pl.when(has_right)
        def _(t=t):
            down(t).start()

        @pl.when(has_left)
        def _(t=t):
            up(t).start()

    for t in range(frames):
        across(frames - 1 - t).start()
        relay(0, t).start()

    for t in range(frames):
        for k in peers:
            spread(k, t).start()

    for t in range(frames):
        for h in range(rows):
            lay_own(t, h + 1, g_ref[t, h])

    def block_of(j):
        return flip(chan // per, j, blocks)

    def produce(n):
        j, k = order[n]
        a, b = pairs[k]
        where = pl.ds(pl.multiple_of(block_of(j) * width, width), width)
        value = None
        for t in range(frames):
            to = t + 2 - a
            if to < frames:
                at = to * deep + (2 - b) * cols
                term = nt(gd[rep, :, at : at + plane], act[0, t, where])
                term = term + nt(gs[:, at : at + plane], act[1, t, where])
                value = term if value is None else value + term
        for i in range(split):
            part[n * split + i] = value[i * piece : (i + 1) * piece]

    def own_edges(t):
        @pl.when(has_left)
        def _():
            down(t).wait_recv()
            down_sib(t).start()

        @pl.when(jnp.logical_not(has_left))
        def _():
            halo[0, t] = jnp.zeros_like(halo[0, t])
            sib_halo[0, t] = jnp.zeros_like(sib_halo[0, t])

        @pl.when(has_right)
        def _():
            up(t).wait_recv()
            up_sib(t).start()

        @pl.when(jnp.logical_not(has_right))
        def _():
            halo[1, t] = jnp.zeros_like(halo[1, t])
            sib_halo[1, t] = jnp.zeros_like(sib_halo[1, t])

        for i in range(2):
            lay_own(t, i * (rows + 1), halo[i, t])

    def sib_edges(t):
        @pl.when(has_left)
        def _():
            down_sib(t).wait_recv()

        @pl.when(has_right)
        def _():
            up_sib(t).wait_recv()

        for i in range(2):
            lay_sib(t, i * (rows + 1), sib_halo[i, t])

    def fetch(j, t):
        for k in range(j * per, (j + 1) * per):
            if quad and k == 3:
                pass_in(0, t).wait_recv()
                pass_in(1, t).wait_recv()
            elif k:
                spread(k, t).wait_recv()
            if k:
                relay(k, t).start()
            if quad and k in (1, 2):
                pass_on(k - 1, t).start()

    def settle(j, t):
        for k in range(j * per, (j + 1) * per):
            relay(k, t).wait_recv()

    middle = n_s // 2
    on_left = space < middle
    inner = jnp.where(on_left, space + 1, space - 1)
    outer = jnp.clip(jnp.where(on_left, space - 1, space + 1), 0, n_s - 1)
    depth = jnp.where(on_left, space, n_s - 1 - space)
    gap = jnp.where(on_left, middle - 1 - space, space - middle)
    central = gap == 0
    has_outer = depth > 0
    deepest = max(middle - 1, n_s - 1 - middle, 0)
    box = jnp.where(central, 1, 0)

    def send_sum(q):
        return remote(sums.at[q], inbox.at[box, q], s_send, s_recv.at[box, q], space=inner)

    def from_outer(q):
        return remote(sums.at[q], inbox.at[0, q], s_send, s_recv.at[0, q], space=inner)

    def from_peer(q):
        return remote(sums.at[q], inbox.at[1, q], s_send, s_recv.at[1, q], space=inner)

    def send_done(q):
        return remote(total.at[q], total.at[q], f_send, f_recv.at[q], space=outer)


    def live(q):
        return jnp.logical_and(q >= 0, q < pieces)

    def tick(time):
        sum_piece = time - LAG_SUM * depth
        done_piece = time - LAG_SUM * deepest - LAG_DONE * (1 + gap)

        @pl.when(live(sum_piece))
        def _():
            @pl.when(has_outer)
            def _():
                from_outer(sum_piece).wait_recv()
                sums[sum_piece] = (part[sum_piece] + inbox[0, sum_piece].astype(F32)).astype(BF16)

            @pl.when(jnp.logical_not(has_outer))
            def _():
                sums[sum_piece] = part[sum_piece].astype(BF16)

            if n_s > 1:
                send_sum(sum_piece).start()

        @pl.when(jnp.logical_and(jnp.logical_or(central, has_outer), live(done_piece)))
        def _():
            @pl.when(central)
            def _():
                value = sums[done_piece]
                if n_s > 1:
                    from_peer(done_piece).wait_recv()
                    value = (value.astype(F32) + inbox[1, done_piece].astype(F32)).astype(BF16)
                total[done_piece] = value

            @pl.when(jnp.logical_not(central))
            def _():
                send_done(done_piece).wait_recv()

            @pl.when(has_outer)
            def _():
                send_done(done_piece).start()

    four = n_s == 4

    def near(q):
        sums[q] = part[q].astype(BF16)
        from_outer(q).start()

    def relayed(q):
        if 0 <= q < pieces:
            from_outer(q).wait_recv()
            sums[q] = (part[q] + inbox[0, q].astype(F32)).astype(BF16)
            from_peer(q).start()
        q = q - LAG_DONE
        if 0 <= q < pieces:
            from_peer(q).wait_recv()
            total[q] = (sums[q].astype(F32) + inbox[1, q].astype(F32)).astype(BF16)
            send_done(q).start()

    def ticks(start, end):
        if not four:
            for time in range(start, end):
                tick(time)
            return

        @pl.when(central)
        def _():
            for time in range(start, end):
                relayed(time - LAG_SUM)

        if start < pieces:
            @pl.when(jnp.logical_not(central))
            def _():
                for time in range(start, min(end, pieces)):
                    near(time)

    def each(start, end, body):
        def run(i, carry):
            body(i)
            return carry

        lax.fori_loop(start, end, run, 0)

    def last(q):
        send_done(q).wait_recv()

    calm = list(range(1, rows - 1))
    rim = [h for h in (0, rows - 1) if h not in calm]
    ranks = calm + rim[: 1 if rows == 1 else 2]

    def line_up(t, some):
        for b in range(3):
            for h in some:
                at = t * deep + (h + 2 - b) * cols
                to = ranks.index(h) * cols
                g3[t, b * 6 * half : (b + 1) * 6 * half, to : to + cols] = gd[:, :, at : at + cols].reshape(6 * half, cols)

    def input_grad(t, some):
        where = slice(ranks.index(some[0]) * cols, (ranks.index(some[-1]) + 1) * cols)
        value = None
        for a in range(first, 3):
            to = t + 2 - a
            if to < frames:
                term = nn(wt_ref[a - first], g3[to, :, where])
                value = term if value is None else value + term
        d_acc[t, :, where] = value
        d_out[t, :, where] = value.astype(BF16)

    def give(t, k):
        return remote(d_out.at[t, chan_rows(k)], d_one.at[t, k], d_send.at[t, k], d_recv.at[t, k], chan=flip(chan, k, n_c))

    def hop(t):
        return 1 + t % 2

    def give_one(t, k):
        block = hop(t) if k == 0 else 3
        return remote(
            d_out.at[t, chan_rows(block)], d_one.at[t, k], d_send.at[t, k], d_recv.at[t, k],
            chan=flip(chan, hop(t), n_c),
        )

    def give_two(t):
        return remote(d_mid.at[t], d_two.at[t], d_send.at[t, 2], d_recv.at[t, 2], chan=flip(chan, 3 - hop(t), n_c))

    def input_send(t):
        if quad:
            give_one(t, 1).start()
            give_one(t, 0).start()
        else:
            for k in peers:
                give(t, k).start()

    def input_mid(t):
        if quad:
            give_one(t, 1).wait_recv()
            d_mid[t] = (d_acc[t, chan_rows(3 - hop(t))] + d_one[t, 1].astype(F32)).astype(BF16)
            give_two(t).start()

    def input_end(t):
        if quad:
            give_one(t, 0).wait_recv()
            give_two(t).wait_recv()
        else:
            for k in peers:
                give(t, k).wait_recv()
        for h in range(rows):
            at = slice(ranks.index(h) * cols, (ranks.index(h) + 1) * cols)
            value = d_acc[t, my_rows, at]
            if quad:
                value = value + d_one[t, 0, :, at].astype(F32) + d_two[t, :, at].astype(F32)
            else:
                for k in peers:
                    value = value + d_one[t, k, :, at].astype(F32)
            v = x_ref[t, h].astype(F32)
            s = jax.nn.sigmoid(v)
            gi_ref[t, h] = (value * (s * (1.0 + v * (1.0 - s)))).astype(BF16)

    def input_sent(t):
        if quad:
            give_one(t, 0).wait_send()
            give_one(t, 1).wait_send()
            give_two(t).wait_send()
        else:
            for k in peers:
                give(t, k).wait_send()

    def inside(t):
        across(t).wait_recv()
        for h in range(rows):
            lay_sib(t, h + 1, sib_rows[t, h])

    def turn(low, high):
        for tap in range(low, high):
            a, b = tap // 3, tap % 3
            wt_ref[a, :, b * 6 * half : (b + 1) * 6 * half] = w_ref[:, tap * 3 : tap * 3 + 3].reshape(6 * half, in_all).T

    before = {}
    turned = (3 - first) * 3
    loads[2].wait()
    loads[3].wait()
    turn(0, turned // 2)

    def at_unit(n, act_now):
        before.setdefault(n, []).append(act_now)

    def grad_part(some, send):
        if some:
            for t in range(frames):
                line_up(t, some)
            for t in reversed(range(frames)):
                input_grad(t, some)
        if send:
            for t in reversed(range(frames)):
                input_send(t)

    ends = jnp.logical_not(jnp.logical_or(central, has_outer))

    at_unit(0, functools.partial(inside, frames - 1))
    at_unit(0, functools.partial(settle, 0, 0))
    for t in range(1, frames):
        at_unit(1, functools.partial(inside, frames - 1 - t))
        at_unit(1, functools.partial(settle, 0, t))
    count = len(pairs)
    plain = 3 - first
    for t in reversed(range(1, frames)):
        at_unit(plain, functools.partial(own_edges, t))
    at_unit(plain, functools.partial(turn, turned // 2, turned))
    at_unit(plain, functools.partial(grad_part, calm, False))
    at_unit(plain, functools.partial(own_edges, 0))

    def inner_rim():
        pl.when(jnp.logical_not(ends))(functools.partial(grad_part, rim, True))

    def end_rim():
        pl.when(ends)(functools.partial(grad_part, rim, True))

    at_unit(plain, inner_rim)
    for t in reversed(range(1, frames)):
        at_unit(plain, functools.partial(sib_edges, t))
    at_unit(plain + 2 * (plain - 1), functools.partial(sib_edges, 0))
    at_unit(count - 1, end_rim)
    if quad:
        for t in range(frames):
            early = t < frames - 1
            for j in (1, 2):
                at_unit(count - 1 if early else count + 3, functools.partial(fetch, j, t))
            for j in (1, 2):
                at_unit(count if early else 2 * count, functools.partial(settle, j, t))
            at_unit(2 * count + 3, functools.partial(fetch, 3, t))
            at_unit(3 * count, functools.partial(settle, 3, t))
    else:
        for j in range(1, blocks):
            for t in range(frames):
                at_unit(j * count, functools.partial(fetch, j, t))
            for t in range(frames):
                at_unit(j * count, functools.partial(settle, j, t))
    for t in reversed(range(frames)):
        at_unit(units - 4, functools.partial(input_mid, t))

    for n in range(units):
        for act_now in before.get(n, []):
            act_now()
        produce(n)
        ticks(n * split, (n + 1) * split)
    if four:
        ticks(pieces, pieces + LAG_SUM + LAG_DONE)
    else:
        each(pieces, pieces + LAG_SUM * deepest + LAG_DONE * (1 + deepest), tick)
    for t in reversed(range(frames)):
        input_end(t)

    @pl.when(ends)
    def _():
        each(0, pieces, last)


    for t in range(frames):
        @pl.when(has_right)
        def _(t=t):
            down(t).wait_send()
            up_sib(t).wait_send()

        @pl.when(has_left)
        def _(t=t):
            up(t).wait_send()
            down_sib(t).wait_send()

        across(t).wait_send()
        for k in range(n_c):
            relay(k, t).wait_send()
        for k in peers:
            spread(k, t).wait_send()
        if quad:
            pass_on(0, t).wait_send()
            pass_on(1, t).wait_send()
        input_sent(t)
    if n_s > 1:
        remote(sums, inbox.at[0], s_send, s_recv.at[0, 0], space=inner).wait_send()

    @pl.when(has_outer)
    def _():
        remote(total, total, f_send, f_recv.at[0], space=outer).wait_send()


def write(cfg, gi_ref, total, gi_out, gw_out, stage, blank, sem):
    n_c, n_s, frames, rows, in_part, out_part, cols, in_all = cfg
    half, width, blocks, per, chunk, split = sizes_of(cfg)
    pairs = taps_of(frames)
    order = order_of(cfg)
    first = max(0, 3 - frames)
    chan = lax.axis_index("chan")
    ranked = sorted(range(len(order)), key=lambda n: (order[n][1], n))
    blank[...] = jnp.zeros_like(blank)
    copies = []
    for i in range(first * 3):
        copies.append(pltpu.make_async_copy(blank, gw_out.at[pl.ds(i * 3, 3)], sem.at[1 + i]))
        copies[-1].start()
    for i, n in enumerate(ranked):
        j, k = order[n]
        a, b = pairs[k]
        where = pl.ds(pl.multiple_of(flip(chan // per, j, blocks) * width, width), width)
        value = total[n * split : (n + 1) * split].astype(F32) * (1.0 / 256.0)
        stage[k, :, :, where] = value.reshape(3, half, width)
        if (i + 1) % blocks == 0:
            copies.append(pltpu.make_async_copy(stage.at[k], gw_out.at[pl.ds((a * 3 + b) * 3, 3)], sem.at[1 + a * 3 + b]))
            copies[-1].start()
    copies.append(pltpu.make_async_copy(gi_ref, gi_out, sem.at[0]))
    copies[-1].start()
    for copy in copies:
        copy.wait()


def on_device(sizes, inputs, grad_out, weight):
    n_c, n_s = sizes
    _, frames, rows, in_part, cols = inputs.shape
    out_part = grad_out.shape[3]
    in_all = weight.shape[4]
    cfg = (n_c, n_s, frames, rows, in_part, out_part, cols, in_all)
    half, width, blocks, per, chunk, split = sizes_of(cfg)
    pairs = taps_of(frames)
    taps = len(pairs) * 3
    plane = rows * cols
    lanes = frames * (rows + 2) * cols
    units = blocks * len(pairs)
    slots = max(3, n_c)
    dma = pltpu.SemaphoreType.DMA
    pieces = units * split
    pile = (pieces, chunk // split, width)
    vmem = pl.BlockSpec(memory_space=pltpu.VMEM)
    hbm = pl.BlockSpec(memory_space=pltpu.HBM)
    grad_in, total = pl.pallas_call(
        functools.partial(kernel, cfg),
        out_shape=(
            jax.ShapeDtypeStruct((frames, rows, in_part, cols), BF16),
            jax.ShapeDtypeStruct(pile, BF16),
        ),
        in_specs=[vmem, hbm],
        out_specs=(vmem, vmem),
        scratch_shapes=[
            pltpu.VMEM((2, taps, half, in_all), BF16),
            pltpu.VMEM((taps // 9, in_all, 18 * half), BF16),
            pltpu.VMEM((frames, 18 * half, plane), BF16),
            pltpu.VMEM((2, frames, in_all, plane), BF16),
            pltpu.VMEM((2, frames, out_part, cols), BF16),
            pltpu.VMEM((2, frames, half, cols), BF16),
            pltpu.VMEM((frames, rows, half, cols), BF16),
            pltpu.VMEM((2, 3 * half, lanes), BF16),
            pltpu.VMEM((3 * half, lanes), BF16),
            pltpu.VMEM(pile, F32),
            pltpu.VMEM(pile, BF16),
            pltpu.VMEM((2,) + pile, BF16),
            pltpu.VMEM((frames, in_all, plane), F32),
            pltpu.VMEM((frames, in_all, plane), BF16),
            pltpu.VMEM((frames, slots, in_part, plane), BF16),
            pltpu.VMEM((frames, in_part, plane), BF16),
            pltpu.VMEM((frames, in_part, plane), BF16),
            dma((4,)),
            dma((4, frames)),
            dma((4, frames)),
            dma((frames,)),
            dma((frames,)),
            dma((n_c, frames)),
            dma((n_c, frames)),
            dma((2, frames)),
            dma((2, frames)),
            dma((n_c, frames)),
            dma((n_c, frames)),
            dma,
            dma((2, pieces)),
            dma,
            dma((pieces,)),
            dma((frames, slots)),
            dma((frames, slots)),
        ],
        compiler_params=pltpu.CompilerParams(
            collective_id=0, has_side_effects=True, vmem_limit_bytes=50 << 20
        ),
    )(
        jnp.stack([inputs.reshape(frames, rows, in_part, cols), grad_out.reshape(frames, rows, out_part, cols)]),
        weight.reshape(27, 2, half, in_all),
    )
    grad_in, grad_weight = pl.pallas_call(
        functools.partial(write, cfg),
        out_shape=(
            jax.ShapeDtypeStruct((frames, rows, in_part, cols), BF16),
            jax.ShapeDtypeStruct((27, half, in_all), F32),
        ),
        in_specs=[vmem, vmem],
        out_specs=(hbm, hbm),
        scratch_shapes=[
            pltpu.VMEM((len(pairs), 3, half, in_all), F32),
            pltpu.VMEM((3, half, in_all), F32),
            dma((10,)),
        ],
        compiler_params=pltpu.CompilerParams(vmem_limit_bytes=50 << 20),
    )(grad_in, total)
    return grad_in.reshape(inputs.shape), grad_weight.reshape(3, 3, 3, half, in_all)


def solution(mesh):
    return jax.shard_map(
        functools.partial(on_device, (mesh.shape["chan"], mesh.shape["space"])),
        mesh=mesh,
        in_specs=(
            P("rep", None, "space", "chan", None),
            P("rep", None, "space", "chan", None),
            P(None, None, None, "chan", None),
        ),
        out_specs=(
            P("rep", None, "space", "chan", None),
            P(None, None, None, ("chan", "rep"), None),
        ),
        check_vma=False,
    )
```

```python
import functools

import jax
import jax.numpy as jnp
from jax import lax
from jax.experimental import pallas as pl
from jax.experimental.pallas import tpu as pltpu
from jax.sharding import PartitionSpec as P

MESH = pl.DeviceIdType.MESH
F32 = jnp.float32
BF16 = jnp.bfloat16
LANES = 128
LAG_SUM = 4
LAG_DONE = 6


def flip(index, mask, count):
    out, bit = 0, 1
    while bit < count:
        out = out + (((index // bit) + ((mask // bit) % 2)) % 2) * bit
        bit *= 2
    return out


def nt(a, b):
    return lax.dot_general(a, b, (((1,), (1,)), ((), ())), preferred_element_type=F32)


def nn(a, b):
    return lax.dot_general(a, b, (((1,), (0,)), ((), ())), preferred_element_type=F32)


def taps_of(frames):
    taps = range(max(0, 3 - frames), 3)
    return [(a, 1) for a in taps] + [(a, b) for a in taps for b in (0, 2)]


def sizes_of(cfg):
    n_c, n_s, frames, rows, in_part, out_part, cols, in_all = cfg
    half = out_part // 2
    width = max(LANES, in_part)
    blocks = in_all // width
    chunk = 3 * half
    split = 2 if chunk % 32 == 0 else 1
    return half, width, blocks, width // in_part, chunk, split


def order_of(cfg):
    half, width, blocks, per, chunk, split = sizes_of(cfg)
    pairs = taps_of(cfg[2])
    every = range(len(pairs))
    if cfg[0] != 4:
        return [(j, k) for j in range(blocks) for k in every]
    low = [k for k in every if pairs[k][0] < 2]
    high = [k for k in every if pairs[k][0] == 2]
    order = [(0, k) for k in every]
    for group in ((1, 2), (3,)):
        for part in (low, high):
            order += [(j, k) for j in group for k in part]
    return order


def kernel(
    cfg,
    xg_ref, w_hbm,
    gi_ref, total,
    w_ref, wt_ref, g3, act, halo, sib_halo, sib_rows, gd, gs,
    part, sums, inbox, d_acc, d_out, d_one, d_two, d_mid,
    in_sem, g_send, g_recv, c_send, c_recv, a_send, a_recv, p_send, p_recv, b_send, b_recv,
    s_send, s_recv, f_send, f_recv, d_send, d_recv,
):
    n_c, n_s, frames, rows, in_part, out_part, cols, in_all = cfg
    half, width, blocks, per, chunk, split = sizes_of(cfg)
    pairs = taps_of(frames)
    order = order_of(cfg)
    first = max(0, 3 - frames)
    plane = rows * cols
    deep = (rows + 2) * cols
    units = len(order)
    pieces = units * split
    piece = chunk // split
    quad = n_c == 4

    x_ref, g_ref = xg_ref.at[0], xg_ref.at[1]
    chan = lax.axis_index("chan")
    space = lax.axis_index("space")
    rep = lax.axis_index("rep")
    other = 1 - rep
    has_left = space > 0
    has_right = space < n_s - 1
    after = (space + 1) % n_s
    below = (space + n_s - 1) % n_s

    def remote(src, dst, ssem, rsem, **where):
        return pltpu.make_async_remote_copy(
            src_ref=src, dst_ref=dst, send_sem=ssem, recv_sem=rsem,
            device_id=where, device_id_type=MESH,
        )

    loads = [
        None, None,
    ] + [
        pltpu.make_async_copy(w_hbm.at[pl.ds(first * 9, (3 - first) * 9), i], w_ref.at[i], in_sem.at[2 + i])
        for i in range(2)
    ]
    for load in loads[2:]:
        load.start()

    barrier = pltpu.get_barrier_semaphore()

    def greet(**where):
        pl.semaphore_signal(barrier, inc=1, device_id=where, device_id_type=MESH)

    peers = (1, 2) if quad else tuple(range(1, n_c))
    for k in peers:
        greet(chan=flip(chan, k, n_c))
    greet(rep=other)

    @pl.when(has_left)
    def _():
        greet(space=below)

    @pl.when(has_right)
    def _():
        greet(space=after)

    my_rows = pl.ds(pl.multiple_of(chan * in_part, in_part), in_part)
    for t in range(frames):
        for h in range(rows):
            v = x_ref[t, h].astype(F32)
            at = h * cols
            act[0, t, my_rows, at : at + cols] = (v * jax.nn.sigmoid(v)).astype(BF16)

    def shifts(row):
        v = row.astype(F32)
        lane = lax.broadcasted_iota(jnp.int32, v.shape, 1)
        ahead = jnp.where(lane < cols - 1, pltpu.roll(v, cols - 1, 1), 0.0)
        behind = jnp.where(lane > 0, pltpu.roll(v, 1, 1), 0.0)
        return ahead.astype(BF16), row, behind.astype(BF16)

    def lay_own(t, p, row):
        at = (t * (rows + 2) + p) * cols
        moved = shifts(row)
        for e in range(3):
            for i in range(2):
                gd[i, e * half : (e + 1) * half, at : at + cols] = moved[e][i * half : (i + 1) * half]

    def lay_sib(t, p, row):
        at = (t * (rows + 2) + p) * cols
        moved = shifts(row)
        for e in range(3):
            gs[e * half : (e + 1) * half, at : at + cols] = moved[e]

    met = len(peers) + 1
    both = jnp.logical_and(has_left, has_right)

    @pl.when(both)
    def _():
        pl.semaphore_wait(barrier, met + 2)

    @pl.when(jnp.logical_not(both))
    def _():
        pl.semaphore_wait(barrier, met + (1 if n_s > 1 else 0))

    theirs = pl.ds(pl.multiple_of(other * half, half), half)

    def across(t):
        return remote(g_ref.at[t, :, theirs], sib_rows.at[t], c_send.at[t], c_recv.at[t], rep=other)

    def down(t):
        return remote(g_ref.at[t, rows - 1], halo.at[0, t], g_send.at[0, t], g_recv.at[0, t], space=after)

    def up(t):
        return remote(g_ref.at[t, 0], halo.at[1, t], g_send.at[1, t], g_recv.at[1, t], space=below)

    def down_sib(t):
        return remote(halo.at[0, t, theirs], sib_halo.at[0, t], g_send.at[2, t], g_recv.at[2, t], rep=other)

    def up_sib(t):
        return remote(halo.at[1, t, theirs], sib_halo.at[1, t], g_send.at[3, t], g_recv.at[3, t], rep=other)

    def chan_rows(k):
        owner = flip(chan, k, n_c)
        return pl.ds(pl.multiple_of(owner * in_part, in_part), in_part)

    def relay(k, t):
        return remote(act.at[0, t, chan_rows(k)], act.at[1, t, chan_rows(k)], b_send.at[k, t], b_recv.at[k, t], rep=other)

    def spread(k, t):
        return remote(act.at[0, t, my_rows], act.at[0, t, my_rows], a_send.at[k, t], a_recv.at[k, t], chan=flip(chan, k, n_c))

    def half_rows(k, i):
        span = in_part // 2
        return pl.ds(pl.multiple_of(flip(chan, k, n_c) * in_part + i * span, span), span)

    def pass_on(i, t):
        where = half_rows(1 + i, i)
        return remote(act.at[0, t, where], act.at[0, t, where], p_send.at[i, t], p_recv.at[i, t], chan=flip(chan, 2 - i, n_c))

    def pass_in(i, t):
        where = half_rows(3, i)
        return remote(act.at[0, t, where], act.at[0, t, where], p_send.at[i, t], p_recv.at[i, t], chan=flip(chan, 2 - i, n_c))

    for t in reversed(range(frames)):
        @pl.when(has_right)
        def _(t=t):
            down(t).start()

        @pl.when(has_left)
        def _(t=t):
            up(t).start()

    for t in range(frames):
        across(frames - 1 - t).start()
        relay(0, t).start()

    for t in range(frames):
        for k in peers:
            spread(k, t).start()

    for t in range(frames):
        for h in range(rows):
            lay_own(t, h + 1, g_ref[t, h])

    def block_of(j):
        return flip(chan // per, j, blocks)

    def produce(n):
        j, k = order[n]
        a, b = pairs[k]
        where = pl.ds(pl.multiple_of(block_of(j) * width, width), width)
        value = None
        for t in range(frames):
            to = t + 2 - a
            if to < frames:
                at = to * deep + (2 - b) * cols
                term = nt(gd[rep, :, at : at + plane], act[0, t, where])
                term = term + nt(gs[:, at : at + plane], act[1, t, where])
                value = term if value is None else value + term
        for i in range(split):
            part[n * split + i] = value[i * piece : (i + 1) * piece]

    def own_edges(t):
        @pl.when(has_left)
        def _():
            down(t).wait_recv()
            down_sib(t).start()

        @pl.when(jnp.logical_not(has_left))
        def _():
            halo[0, t] = jnp.zeros_like(halo[0, t])
            sib_halo[0, t] = jnp.zeros_like(sib_halo[0, t])

        @pl.when(has_right)
        def _():
            up(t).wait_recv()
            up_sib(t).start()

        @pl.when(jnp.logical_not(has_right))
        def _():
            halo[1, t] = jnp.zeros_like(halo[1, t])
            sib_halo[1, t] = jnp.zeros_like(sib_halo[1, t])

        for i in range(2):
            lay_own(t, i * (rows + 1), halo[i, t])

    def sib_edges(t):
        @pl.when(has_left)
        def _():
            down_sib(t).wait_recv()

        @pl.when(has_right)
        def _():
            up_sib(t).wait_recv()

        for i in range(2):
            lay_sib(t, i * (rows + 1), sib_halo[i, t])

    def fetch(j, t):
        for k in range(j * per, (j + 1) * per):
            if quad and k == 3:
                pass_in(0, t).wait_recv()
                pass_in(1, t).wait_recv()
            elif k:
                spread(k, t).wait_recv()
            if k:
                relay(k, t).start()
            if quad and k in (1, 2):
                pass_on(k - 1, t).start()

    def settle(j, t):
        for k in range(j * per, (j + 1) * per):
            relay(k, t).wait_recv()

    middle = n_s // 2
    on_left = space < middle
    inner = jnp.where(on_left, space + 1, space - 1)
    outer = jnp.clip(jnp.where(on_left, space - 1, space + 1), 0, n_s - 1)
    depth = jnp.where(on_left, space, n_s - 1 - space)
    gap = jnp.where(on_left, middle - 1 - space, space - middle)
    central = gap == 0
    has_outer = depth > 0
    deepest = max(middle - 1, n_s - 1 - middle, 0)
    box = jnp.where(central, 1, 0)

    def send_sum(q):
        return remote(sums.at[q], inbox.at[box, q], s_send, s_recv.at[box, q], space=inner)

    def from_outer(q):
        return remote(sums.at[q], inbox.at[0, q], s_send, s_recv.at[0, q], space=inner)

    def from_peer(q):
        return remote(sums.at[q], inbox.at[1, q], s_send, s_recv.at[1, q], space=inner)

    def send_done(q):
        return remote(total.at[q], total.at[q], f_send, f_recv.at[q], space=outer)


    def live(q):
        return jnp.logical_and(q >= 0, q < pieces)

    def tick(time):
        sum_piece = time - LAG_SUM * depth
        done_piece = time - LAG_SUM * deepest - LAG_DONE * (1 + gap)

        @pl.when(live(sum_piece))
        def _():
            @pl.when(has_outer)
            def _():
                from_outer(sum_piece).wait_recv()
                sums[sum_piece] = (part[sum_piece] + inbox[0, sum_piece].astype(F32)).astype(BF16)

            @pl.when(jnp.logical_not(has_outer))
            def _():
                sums[sum_piece] = part[sum_piece].astype(BF16)

            if n_s > 1:
                send_sum(sum_piece).start()

        @pl.when(jnp.logical_and(jnp.logical_or(central, has_outer), live(done_piece)))
        def _():
            @pl.when(central)
            def _():
                value = sums[done_piece]
                if n_s > 1:
                    from_peer(done_piece).wait_recv()
                    value = (value.astype(F32) + inbox[1, done_piece].astype(F32)).astype(BF16)
                total[done_piece] = value

            @pl.when(jnp.logical_not(central))
            def _():
                send_done(done_piece).wait_recv()

            @pl.when(has_outer)
            def _():
                send_done(done_piece).start()

    four = n_s == 4

    def near(q):
        sums[q] = part[q].astype(BF16)
        from_outer(q).start()

    def relayed(q):
        if 0 <= q < pieces:
            from_outer(q).wait_recv()
            sums[q] = (part[q] + inbox[0, q].astype(F32)).astype(BF16)
            from_peer(q).start()
        q = q - LAG_DONE
        if 0 <= q < pieces:
            from_peer(q).wait_recv()
            total[q] = (sums[q].astype(F32) + inbox[1, q].astype(F32)).astype(BF16)
            send_done(q).start()

    def ticks(start, end):
        if not four:
            for time in range(start, end):
                tick(time)
            return

        @pl.when(central)
        def _():
            for time in range(start, end):
                relayed(time - LAG_SUM)

        if start < pieces:
            @pl.when(jnp.logical_not(central))
            def _():
                for time in range(start, min(end, pieces)):
                    near(time)

    def each(start, end, body):
        def run(i, carry):
            body(i)
            return carry

        lax.fori_loop(start, end, run, 0)

    def last(q):
        send_done(q).wait_recv()

    calm = list(range(1, rows - 1))
    rim = [h for h in (0, rows - 1) if h not in calm]
    ranks = calm + rim[: 1 if rows == 1 else 2]

    def line_up(t, some):
        for b in range(3):
            for h in some:
                at = t * deep + (h + 2 - b) * cols
                to = ranks.index(h) * cols
                g3[t, b * 6 * half : (b + 1) * 6 * half, to : to + cols] = gd[:, :, at : at + cols].reshape(6 * half, cols)

    def input_grad(t, some):
        where = slice(ranks.index(some[0]) * cols, (ranks.index(some[-1]) + 1) * cols)
        value = None
        for a in range(first, 3):
            to = t + 2 - a
            if to < frames:
                term = nn(wt_ref[a - first], g3[to, :, where])
                value = term if value is None else value + term
        d_acc[t, :, where] = value
        d_out[t, :, where] = value.astype(BF16)

    def give(t, k):
        return remote(d_out.at[t, chan_rows(k)], d_one.at[t, k], d_send.at[t, k], d_recv.at[t, k], chan=flip(chan, k, n_c))

    def hop(t):
        return 1 + t % 2

    def give_one(t, k):
        block = hop(t) if k == 0 else 3
        return remote(
            d_out.at[t, chan_rows(block)], d_one.at[t, k], d_send.at[t, k], d_recv.at[t, k],
            chan=flip(chan, hop(t), n_c),
        )

    def give_two(t):
        return remote(d_mid.at[t], d_two.at[t], d_send.at[t, 2], d_recv.at[t, 2], chan=flip(chan, 3 - hop(t), n_c))

    def input_send(t):
        if quad:
            give_one(t, 1).start()
            give_one(t, 0).start()
        else:
            for k in peers:
                give(t, k).start()

    def input_mid(t):
        if quad:
            give_one(t, 1).wait_recv()
            d_mid[t] = (d_acc[t, chan_rows(3 - hop(t))] + d_one[t, 1].astype(F32)).astype(BF16)
            give_two(t).start()

    def input_end(t):
        if quad:
            give_one(t, 0).wait_recv()
            give_two(t).wait_recv()
        else:
            for k in peers:
                give(t, k).wait_recv()
        for h in range(rows):
            at = slice(ranks.index(h) * cols, (ranks.index(h) + 1) * cols)
            value = d_acc[t, my_rows, at]
            if quad:
                value = value + d_one[t, 0, :, at].astype(F32) + d_two[t, :, at].astype(F32)
            else:
                for k in peers:
                    value = value + d_one[t, k, :, at].astype(F32)
            v = x_ref[t, h].astype(F32)
            s = jax.nn.sigmoid(v)
            gi_ref[t, h] = (value * (s * (1.0 + v * (1.0 - s)))).astype(BF16)

    def input_sent(t):
        if quad:
            give_one(t, 0).wait_send()
            give_one(t, 1).wait_send()
            give_two(t).wait_send()
        else:
            for k in peers:
                give(t, k).wait_send()

    def inside(t):
        across(t).wait_recv()
        for h in range(rows):
            lay_sib(t, h + 1, sib_rows[t, h])

    def turn(low, high):
        for tap in range(low, high):
            a, b = tap // 3, tap % 3
            wt_ref[a, :, b * 6 * half : (b + 1) * 6 * half] = w_ref[:, tap * 3 : tap * 3 + 3].reshape(6 * half, in_all).T

    before = {}
    turned = (3 - first) * 3
    loads[2].wait()
    loads[3].wait()
    turn(0, turned // 2)

    def at_unit(n, act_now):
        before.setdefault(n, []).append(act_now)

    def grad_part(some, send):
        if some:
            for t in range(frames):
                line_up(t, some)
            for t in reversed(range(frames)):
                input_grad(t, some)
        if send:
            for t in reversed(range(frames)):
                input_send(t)

    ends = jnp.logical_not(jnp.logical_or(central, has_outer))

    at_unit(0, functools.partial(inside, frames - 1))
    at_unit(0, functools.partial(settle, 0, 0))
    for t in range(1, frames):
        at_unit(1, functools.partial(inside, frames - 1 - t))
        at_unit(1, functools.partial(settle, 0, t))
    count = len(pairs)
    plain = 3 - first
    for t in reversed(range(1, frames)):
        at_unit(plain, functools.partial(own_edges, t))
    at_unit(plain, functools.partial(turn, turned // 2, turned))
    at_unit(plain, functools.partial(grad_part, calm, False))
    at_unit(plain, functools.partial(own_edges, 0))

    def inner_rim():
        pl.when(jnp.logical_not(ends))(functools.partial(grad_part, rim, True))

    def end_rim():
        pl.when(ends)(functools.partial(grad_part, rim, True))

    at_unit(plain, inner_rim)
    for t in reversed(range(1, frames)):
        at_unit(plain, functools.partial(sib_edges, t))
    at_unit(plain + 2 * (plain - 1), functools.partial(sib_edges, 0))
    at_unit(count - 1, end_rim)
    if quad:
        for t in range(frames):
            early = t < frames - 1
            for j in (1, 2):
                at_unit(count - 1 if early else count + 3, functools.partial(fetch, j, t))
            for j in (1, 2):
                at_unit(count if early else 2 * count, functools.partial(settle, j, t))
            at_unit(2 * count + 3, functools.partial(fetch, 3, t))
            at_unit(3 * count, functools.partial(settle, 3, t))
    else:
        for j in range(1, blocks):
            for t in range(frames):
                at_unit(j * count, functools.partial(fetch, j, t))
            for t in range(frames):
                at_unit(j * count, functools.partial(settle, j, t))
    for t in reversed(range(frames)):
        at_unit(units - 4, functools.partial(input_mid, t))

    for n in range(units):
        for act_now in before.get(n, []):
            act_now()
        produce(n)
        ticks(n * split, (n + 1) * split)
    if four:
        ticks(pieces, pieces + LAG_SUM + LAG_DONE)
    else:
        each(pieces, pieces + LAG_SUM * deepest + LAG_DONE * (1 + deepest), tick)
    for t in reversed(range(frames)):
        input_end(t)

    @pl.when(ends)
    def _():
        each(0, pieces, last)


    for t in range(frames):
        @pl.when(has_right)
        def _(t=t):
            down(t).wait_send()
            up_sib(t).wait_send()

        @pl.when(has_left)
        def _(t=t):
            up(t).wait_send()
            down_sib(t).wait_send()

        across(t).wait_send()
        for k in range(n_c):
            relay(k, t).wait_send()
        for k in peers:
            spread(k, t).wait_send()
        if quad:
            pass_on(0, t).wait_send()
            pass_on(1, t).wait_send()
        input_sent(t)
    if n_s > 1:
        remote(sums, inbox.at[0], s_send, s_recv.at[0, 0], space=inner).wait_send()

    @pl.when(has_outer)
    def _():
        remote(total, total, f_send, f_recv.at[0], space=outer).wait_send()


def write(cfg, gi_ref, total, gi_out, gw_out, stage, blank, sem):
    n_c, n_s, frames, rows, in_part, out_part, cols, in_all = cfg
    half, width, blocks, per, chunk, split = sizes_of(cfg)
    pairs = taps_of(frames)
    order = order_of(cfg)
    first = max(0, 3 - frames)
    chan = lax.axis_index("chan")
    ranked = sorted(range(len(order)), key=lambda n: (order[n][1], n))
    blank[...] = jnp.zeros_like(blank)
    copies = []
    for i in range(first * 3):
        copies.append(pltpu.make_async_copy(blank, gw_out.at[pl.ds(i * 3, 3)], sem.at[1 + i]))
        copies[-1].start()
    for i, n in enumerate(ranked):
        j, k = order[n]
        a, b = pairs[k]
        where = pl.ds(pl.multiple_of(flip(chan // per, j, blocks) * width, width), width)
        value = total[n * split : (n + 1) * split].astype(F32) * (1.0 / 256.0)
        stage[k, :, :, where] = value.reshape(3, half, width)
        if (i + 1) % blocks == 0:
            copies.append(pltpu.make_async_copy(stage.at[k], gw_out.at[pl.ds((a * 3 + b) * 3, 3)], sem.at[1 + a * 3 + b]))
            copies[-1].start()
    copies.append(pltpu.make_async_copy(gi_ref, gi_out, sem.at[0]))
    copies[-1].start()
    for copy in copies:
        copy.wait()


def on_device(sizes, inputs, grad_out, weight):
    n_c, n_s = sizes
    _, frames, rows, in_part, cols = inputs.shape
    out_part = grad_out.shape[3]
    in_all = weight.shape[4]
    cfg = (n_c, n_s, frames, rows, in_part, out_part, cols, in_all)
    half, width, blocks, per, chunk, split = sizes_of(cfg)
    pairs = taps_of(frames)
    taps = len(pairs) * 3
    plane = rows * cols
    lanes = frames * (rows + 2) * cols
    units = blocks * len(pairs)
    slots = max(3, n_c)
    dma = pltpu.SemaphoreType.DMA
    pieces = units * split
    pile = (pieces, chunk // split, width)
    vmem = pl.BlockSpec(memory_space=pltpu.VMEM)
    hbm = pl.BlockSpec(memory_space=pltpu.HBM)
    grad_in, total = pl.pallas_call(
        functools.partial(kernel, cfg),
        out_shape=(
            jax.ShapeDtypeStruct((frames, rows, in_part, cols), BF16),
            jax.ShapeDtypeStruct(pile, BF16),
        ),
        in_specs=[vmem, hbm],
        out_specs=(vmem, vmem),
        scratch_shapes=[
            pltpu.VMEM((2, taps, half, in_all), BF16),
            pltpu.VMEM((taps // 9, in_all, 18 * half), BF16),
            pltpu.VMEM((frames, 18 * half, plane), BF16),
            pltpu.VMEM((2, frames, in_all, plane), BF16),
            pltpu.VMEM((2, frames, out_part, cols), BF16),
            pltpu.VMEM((2, frames, half, cols), BF16),
            pltpu.VMEM((frames, rows, half, cols), BF16),
            pltpu.VMEM((2, 3 * half, lanes), BF16),
            pltpu.VMEM((3 * half, lanes), BF16),
            pltpu.VMEM(pile, F32),
            pltpu.VMEM(pile, BF16),
            pltpu.VMEM((2,) + pile, BF16),
            pltpu.VMEM((frames, in_all, plane), F32),
            pltpu.VMEM((frames, in_all, plane), BF16),
            pltpu.VMEM((frames, slots, in_part, plane), BF16),
            pltpu.VMEM((frames, in_part, plane), BF16),
            pltpu.VMEM((frames, in_part, plane), BF16),
            dma((4,)),
            dma((4, frames)),
            dma((4, frames)),
            dma((frames,)),
            dma((frames,)),
            dma((n_c, frames)),
            dma((n_c, frames)),
            dma((2, frames)),
            dma((2, frames)),
            dma((n_c, frames)),
            dma((n_c, frames)),
            dma,
            dma((2, pieces)),
            dma,
            dma((pieces,)),
            dma((frames, slots)),
            dma((frames, slots)),
        ],
        compiler_params=pltpu.CompilerParams(
            collective_id=0, has_side_effects=True, vmem_limit_bytes=50 << 20
        ),
    )(
        jnp.stack([inputs.reshape(frames, rows, in_part, cols), grad_out.reshape(frames, rows, out_part, cols)]),
        weight.reshape(27, 2, half, in_all),
    )
    grad_in, grad_weight = pl.pallas_call(
        functools.partial(write, cfg),
        out_shape=(
            jax.ShapeDtypeStruct((frames, rows, in_part, cols), BF16),
            jax.ShapeDtypeStruct((27, half, in_all), F32),
        ),
        in_specs=[vmem, vmem],
        out_specs=(hbm, hbm),
        scratch_shapes=[
            pltpu.VMEM((len(pairs), 3, half, in_all), F32),
            pltpu.VMEM((3, half, in_all), F32),
            dma((10,)),
        ],
        compiler_params=pltpu.CompilerParams(vmem_limit_bytes=50 << 20),
    )(grad_in, total)
    return grad_in.reshape(inputs.shape), grad_weight.reshape(3, 3, 3, half, in_all)


def solution(mesh):
    return jax.shard_map(
        functools.partial(on_device, (mesh.shape["chan"], mesh.shape["space"])),
        mesh=mesh,
        in_specs=(
            P("rep", None, "space", "chan", None),
            P("rep", None, "space", "chan", None),
            P(None, None, None, "chan", None),
        ),
        out_specs=(
            P("rep", None, "space", "chan", None),
            P(None, None, None, ("chan", "rep"), None),
        ),
        check_vma=False,
    )
```
